256 devices in a mesh: oct: 256 (over y, x, z, core).
Axes of the slice: x: 4, y: 4, z: 8, core: 2. Of those that a mesh axis runs over, the one named last changes fastest.
Arguments:
- leaf_spectra: bfloat16 [65536, 2016], P('oct'), may hold values from -6 to 6
- leaf_keys: int32 [65536], P('oct'), may hold values from 8 to 393223, as said below
- parent_keys: int32 [16384], P('oct'), may hold values from 1 to 49152, as said below
- child_phase: float32 [8, 1008], replicated, may hold values from -3.140625 to 3.140625
- coarsen: bfloat16 [2, 1008, 1008], replicated, may hold values from -0.0625 to 0.0625
- transfer: bfloat16 [316, 2016], replicated, may hold values from -0.3125 to 0.3125
- vlist_src: int32 [16384, 189], P('oct'), may hold values from -1 to 511, as said below
- vlist_type: int32 [16384, 189], P('oct'), may hold values from 0 to 315
Outputs:
- upward: bfloat16 [16384, 2016], P('oct')
- local_field: bfloat16 [16384, 2016], P('oct')
The draws below stay inside these ranges and needn't reach their ends.
Inputs may be any that keep to these rules, and one draw needn't show every extreme that they name: leaf_keys: strictly increasing. Every leaf_keys // 8 is a value of parent_keys. The leaves of a parent lie on the device that owns it, except that some of the leaves of a device's last parent (at least one, at most two) are the first leaves of the next device; every device but the first begins so, and the last device's parents have all their leaves at home. parent_keys: strictly increasing; every parent has 1 to 8 leaves. `vlist_src`: in each row the live entries come first, then -1. A live entry is the index of a source parent within the target's window: the 512 parents that end with the last parent of the target's block of 64, counted cyclically. Every target has at least 94 live entries, and on every device some target has all 189 live.
All inputs are finite; a program needn't handle non-finite values.
Results may differ from the reference program's by a relative error of at most 0.0058.
Values may be sent and summed in bfloat16 or wider, within the bound.
No kernel may reach another device: no remote copies, remote signals or barrier semaphores. Data moves between devices by JAX's collectives and lax.ppermute only.
A program may use at most 64 MiB of HBM per device.

```python
import math
import jax
import jax.numpy as jnp
from jax import lax

Q = 1008
PAR_DEV = 64
K = 189
OFFS = 316
GROUP = 512
PARENTS = 16384
LEAVES = 65536
N_OCT = 256


def tree_keys(key):
    base_key = jax.random.fold_in(key, 7001)
    key_gap, key_head, key_inner, key_code = jax.random.split(base_key, 4)
    gaps = jax.random.randint(key_gap, (PARENTS,), 1, 4)
    parent_list = jnp.cumsum(gaps).astype(jnp.int32)
    parent_list = (parent_list + 3 * PARENTS - parent_list[PARENTS - 1]).astype(jnp.int32)
    heads = jax.random.randint(key_head, (N_OCT + 1,), 1, 3)
    heads = heads.at[0].set(0).at[N_OCT].set(0)
    inner = jax.random.randint(key_inner, (N_OCT, PAR_DEV + 1), 0, 3)
    inner = inner.at[:, 0].set(0)
    inner = inner.at[:, PAR_DEV].set(heads[:-1] - heads[1:])
    counts = (4 + inner[:, :-1] - inner[:, 1:]).reshape(PARENTS)
    scores = jax.random.randint(key_code, (PARENTS, 8), 0, 1 << 20) * 8 + jnp.arange(8, dtype=jnp.int32)[None, :]
    scores = scores.at[PARENTS - 1, 7].set(-1)
    ranks = jnp.argsort(jnp.argsort(scores, axis=1, stable=True), axis=1, stable=True)
    chosen = ranks < counts[:, None]
    flat_keys = (parent_list[:, None] * 8 + jnp.arange(8, dtype=jnp.int32)[None, :]).reshape(-1)
    positions = jnp.nonzero(chosen.reshape(-1), size=LEAVES)[0]
    return (flat_keys[positions].astype(jnp.int32), parent_list)


def draw_leaf_keys(key, part):
    return tree_keys(key)[0]


def draw_parent_keys(key, part):
    return tree_keys(key)[1]


def draw_vlist_src(key, part):
    key_length, key_value = jax.random.split(jax.random.fold_in(key, 7013))
    lengths = jax.random.randint(key_length, (PARENTS,), K // 2, K + 1)
    lengths = jnp.where(jnp.arange(PARENTS) % PAR_DEV == 0, K, lengths)
    values = jax.random.randint(key_value, (PARENTS, K), 0, GROUP)
    return jnp.where(jnp.arange(K)[None, :] < lengths[:, None], values, -1).astype(jnp.int32)


def with_ends(drawn, own_key, low, top_value):
    dims = drawn.shape
    index_at = [jax.random.randint(jax.random.fold_in(own_key, axis), (), 0, dims[axis]) for axis in range(len(dims))]
    drawn = drawn.at[tuple(index_at)].set(low)
    longest = dims.index(max(dims))
    index_at[longest] = (index_at[longest] + 1) % dims[longest]
    return drawn.at[tuple(index_at)].set(top_value)


def level_of(rng, extent, cuts, smallest, top_value):
    def one(position, parts):
        heights = jax.random.uniform(jax.random.fold_in(jax.random.fold_in(rng, 6), position), (parts,), jnp.float32, smallest / len(cuts), top_value / len(cuts))
        return jnp.repeat(jnp.exp(heights), extent[position] // parts).reshape((-1,) + (1,) * (len(extent) - position - 1))

    level = one(*cuts[0])
    for cut in cuts[1:]:
        level = level * one(*cut)
    return level


def noise(own_key, dims, width, limit, cuts=(), held_as=jnp.bfloat16):
    entries = jax.random.normal(own_key, dims, jnp.float32) * width
    if len(cuts) > 0:
        entries = level_of(own_key, dims, cuts, -0.22, 0.18) * entries
    return jnp.clip(entries, min=-limit, max=limit).astype(held_as)


def setup_inputs(seed: int = 0) -> dict:
    key_of = jax.random.split(jax.random.key(seed), 9)
    leaf_spectra = noise(key_of[0], (LEAVES, 2 * Q), 1.0, 6.0, ((0, 256),))
    leaf_keys = draw_leaf_keys(jax.random.fold_in(key_of[8], 71), 0)
    parent_keys = draw_parent_keys(jax.random.fold_in(key_of[8], 71), 0)
    child_phase = jnp.clip(jax.random.uniform(key_of[3], (8, Q), jnp.float32, -3.140625, 3.140625), -3.140625, 3.140625)
    coarsen = noise(key_of[4], (2, Q, Q), (8 * Q) ** -0.5, 0.0625)
    transfer = noise(key_of[5], (OFFS, 2 * Q), (2 * K) ** -0.5, 0.3125)
    vlist_src = draw_vlist_src(jax.random.fold_in(key_of[8], 71), 0)
    vlist_type = with_ends(jax.random.randint(key_of[7], (PARENTS, K), 0, OFFS), jax.random.fold_in(key_of[7], 1), 0, OFFS - 1).astype(jnp.int32)
    return {"leaf_spectra": leaf_spectra, "leaf_keys": leaf_keys, "parent_keys": parent_keys, "child_phase": child_phase, "coarsen": coarsen, "transfer": transfer, "vlist_src": vlist_src, "vlist_type": vlist_type}


def twist(leaf_spectra, child_phase, child_code):
    angles = child_phase[child_code]
    cosine = jnp.cos(angles)
    sine_part = jnp.sin(angles)
    spectra = leaf_spectra.astype(jnp.float32)
    real_in = spectra[:, :Q]
    imag_in = spectra[:, Q:]
    return jnp.concatenate([real_in * cosine - imag_in * sine_part, real_in * sine_part + imag_in * cosine], 1)


def coarsen_apply(gathered_b, coarsen):
    real_in = gathered_b[:, :Q]
    imag_in = gathered_b[:, Q:]
    real_out = jnp.dot(real_in, coarsen[0], preferred_element_type=jnp.float32) - jnp.dot(imag_in, coarsen[1], preferred_element_type=jnp.float32)
    imag_out = jnp.dot(real_in, coarsen[1], preferred_element_type=jnp.float32) + jnp.dot(imag_in, coarsen[0], preferred_element_type=jnp.float32)
    return jnp.concatenate([real_out, imag_out], 1).astype(jnp.bfloat16)


def reference(leaf_spectra, leaf_keys, parent_keys, child_phase, coarsen, transfer, vlist_src, vlist_type):
    child_code = leaf_keys % 8
    parent_of = leaf_keys // 8
    twisted = twist(leaf_spectra, child_phase, child_code)
    owner_index = jnp.searchsorted(parent_keys, parent_of).astype(jnp.int32)
    gathered = jax.ops.segment_sum(twisted, owner_index, num_segments=PARENTS)
    gathered_b = gathered.astype(jnp.bfloat16)
    upward = coarsen_apply(gathered_b, coarsen)
    block_rows = math.gcd(PARENTS, 64)
    block_count = PARENTS // block_rows

    def one_block(block_index):
        start = block_index * block_rows
        sources = lax.dynamic_slice_in_dim(vlist_src, start, block_rows, 0)
        kinds = lax.dynamic_slice_in_dim(vlist_type, start, block_rows, 0)
        targets = start + jnp.arange(block_rows, dtype=jnp.int32)
        window_base = (targets // PAR_DEV) * PAR_DEV - GROUP + PAR_DEV
        global_src = (window_base[:, None] + jnp.maximum(sources, 0) + PARENTS) % PARENTS
        live_mask = sources >= 0
        source_rows = upward[global_src.astype(jnp.int32)].astype(jnp.float32)
        coefficient = transfer[kinds].astype(jnp.float32)
        real_part = coefficient[..., :Q] * source_rows[..., :Q] - coefficient[..., Q:] * source_rows[..., Q:]
        imag_part = coefficient[..., :Q] * source_rows[..., Q:] + coefficient[..., Q:] * source_rows[..., :Q]
        products = jnp.concatenate([real_part, imag_part], -1)
        return jnp.sum(jnp.where(live_mask[..., None], products, jnp.float32(0.0)), 1)

    results = lax.map(one_block, jnp.arange(block_count, dtype=jnp.int32))
    local_field = results.reshape(PARENTS, 2 * Q).astype(jnp.bfloat16)
    return upward, local_field
```

```python
import jax
import jax.numpy as jnp
from jax import lax
from jax.experimental import pallas as pl
from jax.experimental.pallas import tpu as pltpu
from jax.sharding import PartitionSpec as P

F32 = jnp.float32
BF16 = jnp.bfloat16
LANES = 128
WINDOW = 8


def lane_of(shape):
    return lax.broadcasted_iota(jnp.int32, shape, 1)


def split_halves(tile_of, half):
    count = -(-half // LANES)
    tail = half - (count - 1) * LANES
    shift = LANES - tail
    total = -(-2 * half // LANES)
    real, imag = [], []
    for k in range(count):
        tile = tile_of(k)
        if k == count - 1:
            tile = jnp.where(lane_of(tile.shape) < tail, tile, 0.0)
        real.append(tile)
        low = pltpu.roll(tile_of(count - 1 + k), shift, 1)
        if count + k < total:
            high = pltpu.roll(tile_of(count + k), shift, 1)
            low = jnp.where(lane_of(low.shape) < shift, low, high)
        if k == count - 1:
            low = jnp.where(lane_of(low.shape) < tail, low, 0.0)
        imag.append(low)
    return real, imag


def join_halves(real, imag, half, store):
    count = -(-half // LANES)
    tail = half - (count - 1) * LANES
    total = -(-2 * half // LANES)
    rolled = [pltpu.roll(tile, tail, 1) for tile in imag]
    for k in range(total):
        width = min(LANES, 2 * half - k * LANES)
        if k < count - 1:
            tile = real[k]
        elif k == count - 1:
            tile = jnp.where(lane_of(real[k].shape) < tail, real[k], rolled[0])
        else:
            j = k - count + 1
            tile = rolled[j - 1]
            if j < count:
                tile = jnp.where(lane_of(tile.shape) < tail, tile, rolled[j])
        store(k, width, tile[:, :width])


def upward_kernel(half, keys_ref, parents_ref, next_keys_ref, next_ref, phase_ref, leaf_hbm, coarsen_hbm,
                  up_ref, rows_ref, leaf_ref, co_ref, cc_ref, ss_ref, g1_ref, g2_ref, lhs_ref, row_ref, sems):
    copies = [
        pltpu.make_async_copy(leaf_hbm, leaf_ref, sems.at[0]),
        pltpu.make_async_copy(coarsen_hbm, co_ref, sems.at[1]),
    ]
    for copy in copies:
        copy.start()
    parents = parents_ref.shape[1]
    cosine = jnp.cos(phase_ref[...])
    sine = jnp.sin(phase_ref[...])
    cc_ref[:, :half] = cosine
    cc_ref[:, half:] = cosine
    ss_ref[:, :half] = sine
    ss_ref[:, half:] = -sine
    parent_row = jnp.broadcast_to(parents_ref[...].astype(F32), (parents, parents))
    diagonal = lax.broadcasted_iota(jnp.int32, (parents, parents), 0) == lane_of((parents, parents))
    parent_col = jnp.sum(jnp.where(diagonal, parent_row, 0.0), axis=1, keepdims=True).astype(jnp.int32)
    keys = keys_ref[...]
    picks = [
        jnp.where(keys == parent_col * 8 + code, 1.0, 0.0).astype(BF16) for code in range(8)
    ]
    picker = jnp.concatenate(picks, 0)
    copies[0].wait()
    total = 2 * half
    for start in range(0, total, 256):
        width = min(256, total - start)
        chosen = jnp.dot(picker, leaf_ref[:, start : start + width], preferred_element_type=F32)
        first = second = None
        for code in range(8):
            part = chosen[code * parents : (code + 1) * parents]
            a = part * cc_ref[code : code + 1, start : start + width]
            b = part * ss_ref[code : code + 1, start : start + width]
            first = a if first is None else first + a
            second = b if second is None else second + b
        g1_ref[:, start : start + width] = first
        g2_ref[:, start : start + width] = second
    last_parent = parents_ref[0, parents - 1]
    add1 = add2 = None
    codes = lax.broadcasted_iota(jnp.int32, (8, total), 0)
    for r in range(next_ref.shape[0]):
        key = next_keys_ref[r]
        mine = lax.shift_right_logical(key, 3) == last_parent
        code = jnp.where(mine, key & 7, 8)
        chosen = codes == code
        spectrum = next_ref[r : r + 1, :].astype(F32)
        a = jnp.sum(jnp.where(chosen, cc_ref[...], 0.0), axis=0, keepdims=True) * spectrum
        b = jnp.sum(jnp.where(chosen, ss_ref[...], 0.0), axis=0, keepdims=True) * spectrum
        add1 = a if add1 is None else add1 + a
        add2 = b if add2 is None else add2 + b
    g1_ref[parents - 1 : parents, :total] += add1
    g2_ref[parents - 1 : parents, :total] += add2
    real1, imag1 = split_halves(lambda k: g1_ref[:, k * LANES : (k + 1) * LANES], half)
    real2, imag2 = split_halves(lambda k: g2_ref[:, k * LANES : (k + 1) * LANES], half)
    for k in range(len(real1)):
        lhs_ref[:parents, k * LANES : (k + 1) * LANES] = (real1[k] + imag2[k]).astype(BF16)
        lhs_ref[parents:, k * LANES : (k + 1) * LANES] = (imag1[k] + real2[k]).astype(BF16)
    copies[1].wait()
    padded = len(real1) * LANES
    real, imag = [], []
    for start in range(0, padded, 256):
        width = min(256, half - start)
        p0 = jnp.dot(lhs_ref[:, :half], co_ref[0, :, start : start + width], preferred_element_type=F32)
        p1 = jnp.dot(lhs_ref[:, :half], co_ref[1, :, start : start + width], preferred_element_type=F32)
        g1_ref[:, start : start + width] = (p0[:parents] - p1[parents:]).astype(BF16).astype(F32)
        g2_ref[:, start : start + width] = (p1[:parents] + p0[parents:]).astype(BF16).astype(F32)
    for k in range(len(real1)):
        tile1 = g1_ref[:, k * LANES : (k + 1) * LANES]
        tile2 = g2_ref[:, k * LANES : (k + 1) * LANES]
        if k == len(real1) - 1:
            inside = lane_of(tile1.shape) < half - k * LANES
            tile1 = jnp.where(inside, tile1, 0.0)
            tile2 = jnp.where(inside, tile2, 0.0)
        real.append(tile1)
        imag.append(tile2)
        for g in range(parents // 8):
            row_ref[pl.ds(g * 128 + k, 8, stride=16), :] = tile1[g * 8 : g * 8 + 8]
            row_ref[pl.ds(g * 128 + 8 + k, 8, stride=16), :] = tile2[g * 8 : g * 8 + 8]

    def store(k, width, tile):
        up_ref[:, k * LANES : k * LANES + width] = tile.astype(BF16)

    join_halves(real, imag, half, store)
    rows_ref[...] = row_ref[...].reshape(parents, 16, LANES).astype(BF16)


def upward_pass(leaf_spectra, leaf_keys, parent_keys, next_keys, next_spectra, child_phase, coarsen):
    half = child_phase.shape[1]
    leaves = leaf_spectra.shape[0]
    parents = parent_keys.shape[0]
    vmem = pl.BlockSpec(memory_space=pltpu.VMEM)
    return pl.pallas_call(
        lambda *refs: upward_kernel(half, *refs),
        out_shape=(
            jax.ShapeDtypeStruct((parents, 2 * half), BF16),
            jax.ShapeDtypeStruct((parents, 16, LANES), BF16),
        ),
        in_specs=[vmem, vmem, pl.BlockSpec(memory_space=pltpu.SMEM), vmem, vmem,
                  pl.BlockSpec(memory_space=pl.ANY), pl.BlockSpec(memory_space=pl.ANY)],
        out_specs=(vmem, vmem),
        scratch_shapes=[
            pltpu.VMEM((leaves, 2 * half), BF16),
            pltpu.VMEM((2, half, half), BF16),
            pltpu.VMEM((8, 2 * half), F32),
            pltpu.VMEM((8, 2 * half), F32),
            pltpu.VMEM((parents, 2048), F32),
            pltpu.VMEM((parents, 2048), F32),
            pltpu.VMEM((2 * parents, 1024), BF16),
            pltpu.VMEM((parents * 16, LANES), F32),
            pltpu.SemaphoreType.DMA((2,)),
        ],
        compiler_params=pltpu.CompilerParams(vmem_limit_bytes=40 << 20),
        name="upward_pass",
    )(leaf_keys.reshape(1, -1), parent_keys.reshape(1, -1), next_keys, next_spectra, child_phase, leaf_spectra, coarsen)


FIRST = 96
STEP = 24


def interact_kernel(half, src_ref, kind_ref, live_ref, *refs):
    block_refs = refs[:WINDOW]
    transfer_ref, out_ref, table_ref, coef_ref, sum_ref, wide_ref = refs[WINDOW:]
    targets = out_ref.shape[0]
    rows = block_refs[0].shape[0]
    zero_row = WINDOW * rows
    for w in range(WINDOW):
        def widen(i, _, w=w):
            table_ref[w * rows + i] = block_refs[w][i].astype(F32)
            return 0
        lax.fori_loop(0, rows, widen, 0, unroll=8)
    table_ref[zero_row] = jnp.zeros((16, LANES), F32)

    def lay_out(start, count):
        wide_ref[:count, : 2 * half] = transfer_ref[pl.ds(start, count), :].astype(F32)
        real, imag = split_halves(lambda k: wide_ref[:count, k * LANES : (k + 1) * LANES], half)
        for k in range(len(real)):
            for g in range(0, count, 8):
                size = min(8, count - g)
                coef_ref[pl.ds((start + g) * 16 + k, size, stride=16), :] = real[k][g : g + size]
                coef_ref[pl.ds((start + g) * 16 + 8 + k, size, stride=16), :] = imag[k][g : g + size]

    kinds = transfer_ref.shape[0]
    whole = kinds // 16

    def lay_out_step(i, _):
        lay_out(pl.multiple_of(i * 16, 16), 16)
        return 0

    lax.fori_loop(0, whole, lay_out_step, 0)
    if kinds % 16:
        lay_out(whole * 16, kinds % 16)

    def one_target(j, _):
        def some(base, count, carry):
            carry = list(carry)
            for u in range(count):
                s = src_ref[j, base + u]
                t = pl.multiple_of(kind_ref[j, base + u] * 16, 16)
                sr = table_ref[s, 0:8, :]
                si = table_ref[s, 8:16, :]
                cr = coef_ref[pl.ds(t, 8), :]
                ci = coef_ref[pl.ds(t + 8, 8), :]
                p = 2 * (u % 2)
                carry[p] = carry[p] + (cr * sr - ci * si)
                carry[p + 1] = carry[p + 1] + (cr * si + ci * sr)
            return tuple(carry)

        zero = jnp.zeros((8, LANES), F32)
        carry = some(0, FIRST, (zero,) * 4)
        steps = lax.div(live_ref[j] - FIRST + (STEP - 1), STEP)
        carry = lax.fori_loop(0, steps, lambda i, c: some(FIRST + i * STEP, STEP, c), carry)
        base = pl.multiple_of(j * 16, 16)
        sum_ref[pl.ds(base, 8), :] = carry[0] + carry[2]
        sum_ref[pl.ds(base + 8, 8), :] = carry[1] + carry[3]
        return 0

    lax.fori_loop(0, targets, one_target, 0)
    count = -(-half // LANES)
    real, imag = [], []
    for k in range(count):
        real.append(jnp.concatenate([sum_ref[pl.ds(g * 128 + k, 8, stride=16), :] for g in range(targets // 8)], 0))
        imag.append(jnp.concatenate([sum_ref[pl.ds(g * 128 + 8 + k, 8, stride=16), :] for g in range(targets // 8)], 0))

    def store(k, width, tile):
        out_ref[:, k * LANES : k * LANES + width] = tile.astype(BF16)

    join_halves(real, imag, half, store)


def interact(blocks, src, kind, live, transfer):
    half = transfer.shape[1] // 2
    targets = src.shape[0]
    rows = blocks[0].shape[0]
    vmem = pl.BlockSpec(memory_space=pltpu.VMEM)
    smem = pl.BlockSpec(memory_space=pltpu.SMEM)
    return pl.pallas_call(
        lambda *refs: interact_kernel(half, *refs),
        out_shape=jax.ShapeDtypeStruct((targets, 2 * half), BF16),
        in_specs=[smem, smem, smem] + [vmem] * WINDOW + [vmem],
        out_specs=vmem,
        scratch_shapes=[
            pltpu.VMEM((WINDOW * rows + 8, 16, LANES), F32),
            pltpu.VMEM((320 * 16, LANES), F32),
            pltpu.VMEM((targets * 16, LANES), F32),
            pltpu.VMEM((16, 2048), F32),
        ],
        compiler_params=pltpu.CompilerParams(vmem_limit_bytes=40 << 20),
        name="interact",
    )(src, kind, live, *blocks, transfer)


def shards(leaf_spectra, leaf_keys, parent_keys, child_phase, coarsen, transfer, vlist_src, vlist_type):
    count = lax.axis_size("oct")
    back = [(i, i - 1) for i in range(1, count)]
    next_spectra = lax.ppermute(leaf_spectra[:2], "oct", back)
    next_keys = lax.ppermute(leaf_keys[:2], "oct", back)
    upward, rows = upward_pass(leaf_spectra, leaf_keys, parent_keys, next_keys, next_spectra, child_phase, coarsen)
    blocks = [rows]
    for distance in range(1, WINDOW):
        route = [((i - distance) % count, i) for i in range(count)]
        blocks = [lax.ppermute(rows, "oct", route)] + blocks
    slots = vlist_src.shape[1]
    width = FIRST + -(-(slots - FIRST) // STEP) * STEP
    dead = vlist_src < 0
    live = jnp.sum(jnp.where(dead, 0, 1), axis=1).astype(jnp.int32)
    zero_row = WINDOW * parent_keys.shape[0]
    src = jnp.pad(jnp.where(dead, zero_row, vlist_src), ((0, 0), (0, width - slots)), constant_values=zero_row)
    kind = jnp.pad(vlist_type, ((0, 0), (0, width - slots)))
    local_field = interact(blocks, src, kind, live, transfer)
    return upward, local_field


def solution(mesh):
    return jax.shard_map(
        shards,
        mesh=mesh,
        in_specs=(P("oct", None), P("oct"), P("oct"), P(), P(), P(), P("oct", None), P("oct", None)),
        out_specs=(P("oct", None), P("oct", None)),
        check_vma=False,
    )
```

```python
import jax
import jax.numpy as jnp
from jax import lax
from jax.experimental import pallas as pl
from jax.experimental.pallas import tpu as pltpu
from jax.sharding import PartitionSpec as P

F32 = jnp.float32
BF16 = jnp.bfloat16
LANES = 128
WINDOW = 8
HELD = 4
UNROLL = 8
ROW = 192
DEAD = 1 << 20


def lane_of(shape):
    return lax.broadcasted_iota(jnp.int32, shape, 1)


def split_halves(tile_of, half):
    count = -(-half // LANES)
    tail = half - (count - 1) * LANES
    shift = LANES - tail
    total = -(-2 * half // LANES)
    real, imag = [], []
    for k in range(count):
        tile = tile_of(k)
        if k == count - 1:
            tile = jnp.where(lane_of(tile.shape) < tail, tile, 0.0)
        real.append(tile)
        low = pltpu.roll(tile_of(count - 1 + k), shift, 1)
        if count + k < total:
            high = pltpu.roll(tile_of(count + k), shift, 1)
            low = jnp.where(lane_of(low.shape) < shift, low, high)
        if k == count - 1:
            low = jnp.where(lane_of(low.shape) < tail, low, 0.0)
        imag.append(low)
    return real, imag


def join_halves(real, imag, half, store):
    count = -(-half // LANES)
    tail = half - (count - 1) * LANES
    total = -(-2 * half // LANES)
    rolled = [pltpu.roll(tile, tail, 1) for tile in imag]
    for k in range(total):
        width = min(LANES, 2 * half - k * LANES)
        if k < count - 1:
            tile = real[k]
        elif k == count - 1:
            tile = jnp.where(lane_of(real[k].shape) < tail, real[k], rolled[0])
        else:
            j = k - count + 1
            tile = rolled[j - 1]
            if j < count:
                tile = jnp.where(lane_of(tile.shape) < tail, tile, rolled[j])
        store(k, width, tile[:, :width])


def gather_kernel(half, keys_ref, parents_ref, phase_hbm, leaf_hbm, g1_ref, g2_ref, cc_ref, ss_ref, leaf_ref, phase_ref, sems):
    copies = [
        pltpu.make_async_copy(phase_hbm, phase_ref, sems.at[0]),
        pltpu.make_async_copy(leaf_hbm, leaf_ref, sems.at[1]),
    ]
    for copy in copies:
        copy.start()
    parents = parents_ref.shape[1]
    parent_row = jnp.broadcast_to(parents_ref[...].astype(F32), (parents, parents))
    diagonal = lax.broadcasted_iota(jnp.int32, (parents, parents), 0) == lane_of((parents, parents))
    parent_col = jnp.sum(jnp.where(diagonal, parent_row, 0.0), axis=1, keepdims=True).astype(jnp.int32)
    keys = keys_ref[...]
    picks = [
        jnp.where(keys == parent_col * 8 + code, 1.0, 0.0).astype(BF16) for code in range(8)
    ]
    picker = jnp.concatenate(picks, 0)
    copies[0].wait()
    cosine = jnp.cos(phase_ref[...])
    sine = jnp.sin(phase_ref[...])
    cc_ref[:, :half] = cosine
    cc_ref[:, half:] = cosine
    ss_ref[:, :half] = sine
    ss_ref[:, half:] = -sine
    copies[1].wait()
    total = 2 * half
    for start in range(0, total, 256):
        width = min(256, total - start)
        chosen = jnp.dot(picker, leaf_ref[:, start : start + width], preferred_element_type=F32)
        first = second = None
        for code in range(8):
            part = chosen[code * parents : (code + 1) * parents]
            a = part * cc_ref[code : code + 1, start : start + width]
            b = part * ss_ref[code : code + 1, start : start + width]
            first = a if first is None else first + a
            second = b if second is None else second + b
        g1_ref[:, start : start + width] = first
        g2_ref[:, start : start + width] = second


def upward_kernel(half, parents_ref, next_ref, cc_ref, ss_ref, in1_ref, in2_ref, co_ref,
                  up_ref, rows_ref, g1_ref, g2_ref, lhs_ref, row_ref):
    parents = parents_ref.shape[1]
    total = 2 * half
    g1_ref[...] = in1_ref[...]
    g2_ref[...] = in2_ref[...]
    last_parent = parents_ref[:, parents - 1 : parents]
    add1 = add2 = None
    codes = lax.broadcasted_iota(jnp.int32, (8, 1), 0)
    for r in range(next_ref.shape[0]):
        digits = next_ref[r : r + 1, total : total + 3].astype(F32).astype(jnp.int32)
        key = digits[:, 0:1] * 65536 + digits[:, 1:2] * 256 + digits[:, 2:3]
        chosen = jnp.where(key == last_parent * 8 + codes, 1.0, 0.0)
        spectrum = next_ref[r : r + 1, :total].astype(F32)
        a = jnp.sum(chosen * cc_ref[...], axis=0, keepdims=True) * spectrum
        b = jnp.sum(chosen * ss_ref[...], axis=0, keepdims=True) * spectrum
        add1 = a if add1 is None else add1 + a
        add2 = b if add2 is None else add2 + b
    g1_ref[parents - 1 : parents, :total] += add1
    g2_ref[parents - 1 : parents, :total] += add2
    real1, imag1 = split_halves(lambda k: g1_ref[:, k * LANES : (k + 1) * LANES], half)
    real2, imag2 = split_halves(lambda k: g2_ref[:, k * LANES : (k + 1) * LANES], half)
    for k in range(len(real1)):
        lhs_ref[:parents, k * LANES : (k + 1) * LANES] = (real1[k] + imag2[k]).astype(BF16)
        lhs_ref[parents:, k * LANES : (k + 1) * LANES] = (imag1[k] + real2[k]).astype(BF16)
    padded = len(real1) * LANES
    real, imag = [], []
    for start in range(0, padded, 256):
        width = min(256, half - start)
        p0 = jnp.dot(lhs_ref[:, :half], co_ref[0, :, start : start + width], preferred_element_type=F32)
        p1 = jnp.dot(lhs_ref[:, :half], co_ref[1, :, start : start + width], preferred_element_type=F32)
        g1_ref[:, start : start + width] = (p0[:parents] - p1[parents:]).astype(BF16).astype(F32)
        g2_ref[:, start : start + width] = (p1[:parents] + p0[parents:]).astype(BF16).astype(F32)
    for k in range(len(real1)):
        tile1 = g1_ref[:, k * LANES : (k + 1) * LANES]
        tile2 = g2_ref[:, k * LANES : (k + 1) * LANES]
        if k == len(real1) - 1:
            inside = lane_of(tile1.shape) < half - k * LANES
            tile1 = jnp.where(inside, tile1, 0.0)
            tile2 = jnp.where(inside, tile2, 0.0)
        real.append(tile1)
        imag.append(tile2)
        for g in range(parents // 8):
            row_ref[pl.ds(g * 128 + k, 8, stride=16), :] = tile1[g * 8 : g * 8 + 8]
            row_ref[pl.ds(g * 128 + 8 + k, 8, stride=16), :] = tile2[g * 8 : g * 8 + 8]

    def store(k, width, tile):
        up_ref[:, k * LANES : k * LANES + width] = tile.astype(BF16)

    join_halves(real, imag, half, store)
    rows_ref[...] = row_ref[...].reshape(parents, 16, LANES).astype(BF16)


VM = pl.BlockSpec(memory_space=pltpu.VMEM)
SM = pl.BlockSpec(memory_space=pltpu.SMEM)
HB = pl.BlockSpec(memory_space=pltpu.HBM)


def params(mib):
    return pltpu.CompilerParams(vmem_limit_bytes=mib << 20)


def cost(flops, nbytes):
    return pl.CostEstimate(flops=flops, bytes_accessed=nbytes, transcendentals=0)


def gather_leaves(leaf_spectra, leaf_keys, parent_keys, child_phase):
    half = child_phase.shape[1]
    leaves = leaf_spectra.shape[0]
    parents = parent_keys.shape[1]
    return pl.pallas_call(
        lambda *refs: gather_kernel(half, *refs),
        out_shape=(
            jax.ShapeDtypeStruct((parents, 2048), F32),
            jax.ShapeDtypeStruct((parents, 2048), F32),
            jax.ShapeDtypeStruct((8, 2 * half), F32),
            jax.ShapeDtypeStruct((8, 2 * half), F32),
        ),
        in_specs=[VM, VM, HB, HB],
        out_specs=(VM, VM, VM, VM),
        scratch_shapes=[
            pltpu.VMEM((leaves, 2 * half), BF16),
            pltpu.VMEM((8, half), F32),
            pltpu.SemaphoreType.DMA((2,)),
        ],
        compiler_params=params(12),
        cost_estimate=cost(8 << 28, 6 << 20),
        name="gather_leaves",
    )(leaf_keys, parent_keys, child_phase, leaf_spectra)


def upward_pass(parent_keys, following, cosines, sines, first, second, coarsen):
    half = coarsen.shape[1]
    parents = parent_keys.shape[1]
    return pl.pallas_call(
        lambda *refs: upward_kernel(half, *refs),
        out_shape=(
            jax.ShapeDtypeStruct((parents, 2 * half), BF16),
            jax.ShapeDtypeStruct((parents, 16, LANES), BF16),
        ),
        in_specs=[VM] * 7,
        out_specs=(VM, VM),
        scratch_shapes=[
            pltpu.VMEM((parents, 2048), F32),
            pltpu.VMEM((parents, 2048), F32),
            pltpu.VMEM((2 * parents, 1024), BF16),
            pltpu.VMEM((parents * 16, LANES), F32),
        ],
        compiler_params=params(12),
        cost_estimate=cost(8 << 28, 6 << 20),
        name="upward_pass",
    )(parent_keys, following, cosines, sines, first, second, coarsen)


def coefficient_kernel(half, transfer_ref, coef_ref, wide_ref):
    def lay_out(start, count):
        wide_ref[:count, : 2 * half] = transfer_ref[pl.ds(start, count), :].astype(F32)
        real, imag = split_halves(lambda k: wide_ref[:count, k * LANES : (k + 1) * LANES], half)
        for k in range(len(real)):
            for g in range(0, count, 8):
                size = min(8, count - g)
                coef_ref[pl.ds((start + g) * 16 + k, size, stride=16), :] = real[k][g : g + size]
                coef_ref[pl.ds((start + g) * 16 + 8 + k, size, stride=16), :] = imag[k][g : g + size]

    kinds = transfer_ref.shape[0]
    whole = kinds // 16

    def lay_out_step(i, _):
        lay_out(pl.multiple_of(i * 16, 16), 16)
        return 0

    lax.fori_loop(0, whole, lay_out_step, 0)
    if kinds % 16:
        lay_out(whole * 16, kinds % 16)


def coefficient_rows(transfer):
    kinds, width = transfer.shape
    return pl.pallas_call(
        lambda *refs: coefficient_kernel(width // 2, *refs),
        out_shape=jax.ShapeDtypeStruct((kinds * 16, LANES), F32),
        in_specs=[VM],
        out_specs=VM,
        scratch_shapes=[pltpu.VMEM((16, 2048), F32)],
        compiler_params=params(8),
        cost_estimate=cost(8 << 28, 6 << 20),
        name="coefficient_rows",
    )(transfer)


def interact_kernel(src_ref, kind_ref, live_ref, *refs):
    block_refs = refs[:HELD]
    coef_ref, out_ref, table_ref = refs[HELD:]
    targets = out_ref.shape[0]
    rows = block_refs[0].shape[0]
    for w in range(HELD):
        def widen(i, _, w=w):
            base = pl.multiple_of(w * rows * 16 + i * 16, 16)
            table_ref[pl.ds(base, 16), :] = block_refs[w][i].astype(F32)
            return 0
        lax.fori_loop(0, rows, widen, 0, unroll=8)
    table_ref[HELD * rows * 16 : HELD * rows * 16 + 16, :] = jnp.zeros((16, LANES), F32)

    def load(start):
        loaded = []
        for u in range(UNROLL):
            s = pl.multiple_of(src_ref[start + u], 16)
            t = pl.multiple_of(kind_ref[start + u], 16)
            loaded.append(table_ref[pl.ds(s, 8), :])
            loaded.append(table_ref[pl.ds(s + 8, 8), :])
            loaded.append(coef_ref[pl.ds(t, 8), :])
            loaded.append(coef_ref[pl.ds(t + 8, 8), :])
        return tuple(loaded)

    def one_target(j, _):
        base = j * ROW

        def step(i, carry):
            sums, loaded = list(carry[:4]), carry[4:]
            following = load(base + (i + 1) * UNROLL)
            for u in range(UNROLL):
                sr, si, cr, ci = loaded[4 * u : 4 * u + 4]
                p = 2 * (u % 2)
                sums[p] = sums[p] + (cr * sr - ci * si)
                sums[p + 1] = sums[p + 1] + (cr * si + ci * sr)
            return tuple(sums) + following

        zero = jnp.zeros((8, LANES), F32)
        steps = lax.div(live_ref[j] + (UNROLL - 1), UNROLL)
        carry = lax.fori_loop(0, steps, step, (zero,) * 4 + load(base))
        out_ref[j, 0:8, :] = (carry[0] + carry[2]).astype(out_ref.dtype)
        out_ref[j, 8:16, :] = (carry[1] + carry[3]).astype(out_ref.dtype)
        return 0

    lax.fori_loop(0, targets, one_target, 0)


def interact(blocks, src, kind, live, coefs, dtype, name):
    targets = live.shape[0]
    rows = blocks[0].shape[0]
    return pl.pallas_call(
        interact_kernel,
        out_shape=jax.ShapeDtypeStruct((targets, 16, LANES), dtype),
        in_specs=[SM, SM, SM] + [VM] * HELD + [VM],
        out_specs=VM,
        scratch_shapes=[pltpu.VMEM((HELD * rows * 16 + 16, LANES), F32)],
        compiler_params=params(12),
        cost_estimate=cost(8 << 30, 6 << 20),
        name=name,
    )(src, kind, live, *blocks, coefs)


def finish_kernel(half, near_ref, far_ref, out_ref, sum_ref):
    targets = out_ref.shape[0]
    sum_ref[...] = (near_ref[...] + far_ref[...].astype(F32)).reshape(targets * 16, LANES)
    count = -(-half // LANES)
    real, imag = [], []
    for k in range(count):
        real.append(jnp.concatenate([sum_ref[pl.ds(g * 128 + k, 8, stride=16), :] for g in range(targets // 8)], 0))
        imag.append(jnp.concatenate([sum_ref[pl.ds(g * 128 + 8 + k, 8, stride=16), :] for g in range(targets // 8)], 0))

    def store(k, width, tile):
        out_ref[:, k * LANES : k * LANES + width] = tile.astype(BF16)

    join_halves(real, imag, half, store)


def finish(near, far, half):
    targets = near.shape[0]
    return pl.pallas_call(
        lambda *refs: finish_kernel(half, *refs),
        out_shape=jax.ShapeDtypeStruct((targets, 2 * half), BF16),
        in_specs=[VM, VM],
        out_specs=VM,
        scratch_shapes=[pltpu.VMEM((targets * 16, LANES), F32)],
        compiler_params=params(4),
        name="finish",
    )(near, far)


def shifted(value, distance):
    count = lax.axis_size("oct")
    return lax.ppermute(value, "oct", [(i, (i + distance) % count) for i in range(count)])


def shards(leaf_spectra, leaf_keys, parent_keys, child_phase, coarsen, transfer, vlist_src, vlist_type):
    count = lax.axis_size("oct")
    half = child_phase.shape[1]
    parents = parent_keys.shape[0]
    odd = lax.axis_index("oct") % 2 == 1
    head_keys = leaf_keys[:2, None]
    digits = jnp.concatenate([head_keys >> 16, (head_keys >> 8) & 255, head_keys & 255], 1)
    head = jnp.concatenate([leaf_spectra[:2], digits.astype(BF16)], 1)
    following = lax.ppermute(head, "oct", [(i, i - 1) for i in range(1, count)])
    keys_row = leaf_keys.reshape(1, -1)
    parents_row = parent_keys.reshape(1, -1)
    first, second, cosines, sines = gather_leaves(leaf_spectra, keys_row, parents_row, child_phase)
    upward, rows = upward_pass(parents_row, following, cosines, sines, first, second, coarsen)

    behind2 = shifted(rows, 2)
    crossed = lax.ppermute(rows, "oct", [(i, (i + 1 + 2 * (i % 2)) % count) for i in range(count)])
    swapped = lax.ppermute(behind2, "oct", [(i, i ^ 1) for i in range(count)])
    blocks = [crossed, behind2, swapped, rows]

    packed = jnp.where(vlist_src < 0, DEAD, vlist_src * 512 + vlist_type)
    theirs = shifted(packed, -HELD)
    mine = jnp.where(vlist_src < 0, DEAD, (511 - vlist_src) * 512 + vlist_type)
    ordered = jnp.sort(jnp.concatenate([theirs, mine], 0), axis=1)
    ordered = jnp.pad(ordered, ((0, 0), (0, ROW - ordered.shape[1])), constant_values=DEAD)
    held = HELD * parents
    valid = ordered < held * 512
    live = jnp.sum(jnp.where(valid, 1, 0), axis=1).astype(jnp.int32)
    place = ordered >> 9
    is_mine = lax.broadcasted_iota(jnp.int32, place.shape, 0) >= parents
    place = jnp.where(is_mine, held - 1 - place, place)
    place = jnp.where(odd & ((place & parents) == 0), place ^ (2 * parents), place)
    place = jnp.where(valid, place, held) * 16
    kind = jnp.where(valid, ordered & 511, 0) * 16
    place = jnp.pad(place.reshape(-1), (0, 64), constant_values=held * 16)
    kind = jnp.pad(kind.reshape(-1), (0, 64))
    coefs = coefficient_rows(transfer)

    cut = parents * ROW
    far = interact(blocks, place[: cut + 64], kind[: cut + 64], live[:parents], coefs, BF16, "far")
    arrived = shifted(far, HELD)
    near = interact(blocks, place[cut:], kind[cut:], live[parents:], coefs, F32, "near")
    local_field = finish(near, arrived, half)
    return upward, local_field


def solution(mesh):
    return jax.shard_map(
        shards,
        mesh=mesh,
        in_specs=(P("oct", None), P("oct"), P("oct"), P(), P(), P(), P("oct", None), P("oct", None)),
        out_specs=(P("oct", None), P("oct", None)),
        check_vma=False,
    )
```

```python
import jax
import jax.numpy as jnp
from jax import lax
from jax.experimental import pallas as pl
from jax.experimental.pallas import tpu as pltpu
from jax.sharding import PartitionSpec as P


F32 = jnp.float32
BF16 = jnp.bfloat16
LANES = 128
HELD = 4
UNROLL = 16
ROW = 256
DEAD = 1 << 20


def lane_of(shape):
    return lax.broadcasted_iota(jnp.int32, shape, 1)


def split_halves(tile_of, half):
    count = -(-half // LANES)
    tail = half - (count - 1) * LANES
    shift = LANES - tail
    total = -(-2 * half // LANES)
    real, imag = [], []
    for k in range(count):
        tile = tile_of(k)
        if k == count - 1:
            tile = jnp.where(lane_of(tile.shape) < tail, tile, 0.0)
        real.append(tile)
        low = pltpu.roll(tile_of(count - 1 + k), shift, 1)
        if count + k < total:
            high = pltpu.roll(tile_of(count + k), shift, 1)
            low = jnp.where(lane_of(low.shape) < shift, low, high)
        if k == count - 1:
            low = jnp.where(lane_of(low.shape) < tail, low, 0.0)
        imag.append(low)
    return real, imag


def join_halves(real, imag, half, store):
    count = -(-half // LANES)
    tail = half - (count - 1) * LANES
    total = -(-2 * half // LANES)
    rolled = [pltpu.roll(tile, tail, 1) for tile in imag]
    for k in range(total):
        width = min(LANES, 2 * half - k * LANES)
        if k < count - 1:
            tile = real[k]
        elif k == count - 1:
            tile = jnp.where(lane_of(real[k].shape) < tail, real[k], rolled[0])
        else:
            j = k - count + 1
            tile = rolled[j - 1]
            if j < count:
                tile = jnp.where(lane_of(tile.shape) < tail, tile, rolled[j])
        store(k, width, tile[:, :width])


def select_rows(picker, columns):
    return lax.dot_general(picker, columns, (((1,), (1,)), ((), ())), preferred_element_type=F32)


def gather_kernel(half, keys_hbm, parents_hbm, phase_hbm, leaf_hbm, coarsen_hbm,
                  g1_ref, g2_ref, cc_ref, ss_ref, co_ref, keys_ref, parents_ref, leaf_ref, phase_ref, sems):
    copies = [
        pltpu.make_async_copy(src, dst, sems.at[i])
        for i, (src, dst) in enumerate((
            (keys_hbm, keys_ref), (parents_hbm, parents_ref), (phase_hbm, phase_ref),
            (leaf_hbm, leaf_ref), (coarsen_hbm, co_ref),
        ))
    ]
    for copy in copies:
        copy.start()
    copies[0].wait()
    copies[1].wait()
    parents = parents_ref.shape[1]
    parent_row = jnp.broadcast_to(parents_ref[...].astype(F32), (parents, parents))
    diagonal = lax.broadcasted_iota(jnp.int32, (parents, parents), 0) == lane_of((parents, parents))
    parent_col = jnp.sum(jnp.where(diagonal, parent_row, 0.0), axis=1, keepdims=True).astype(jnp.int32)
    keys = keys_ref[...]
    picks = [
        jnp.where(keys == parent_col * 8 + code, 1.0, 0.0).astype(BF16) for code in range(8)
    ]
    picker = jnp.concatenate(picks, 0)
    copies[2].wait()
    cosine = jnp.cos(phase_ref[...])
    sine = jnp.sin(phase_ref[...])
    cc_ref[:, :half] = cosine
    cc_ref[:, half:] = cosine
    ss_ref[:, :half] = sine
    ss_ref[:, half:] = -sine
    copies[3].wait()
    total = 2 * half
    for start in range(0, total, 256):
        width = min(256, total - start)
        chosen = select_rows(picker, leaf_ref[start : start + width, :])
        first = second = None
        for code in range(8):
            part = chosen[code * parents : (code + 1) * parents]
            a = part * cc_ref[code : code + 1, start : start + width]
            b = part * ss_ref[code : code + 1, start : start + width]
            first = a if first is None else first + a
            second = b if second is None else second + b
        g1_ref[:, start : start + width] = first
        g2_ref[:, start : start + width] = second
    copies[4].wait()


def upward_kernel(half, parents_ref, next_ref, cc_ref, ss_ref, in1_ref, in2_ref, co_ref,
                  up_ref, rows_ref, g1_ref, g2_ref, lhs_ref, row_ref):
    parents = parents_ref.shape[1]
    total = 2 * half
    g1_ref[...] = in1_ref[...]
    g2_ref[...] = in2_ref[...]
    last_parent = parents_ref[:, parents - 1 : parents]
    add1 = add2 = None
    codes = lax.broadcasted_iota(jnp.int32, (8, 1), 0)
    for r in range(next_ref.shape[0]):
        digits = next_ref[r : r + 1, total : total + 3].astype(F32).astype(jnp.int32)
        key = digits[:, 0:1] * 65536 + digits[:, 1:2] * 256 + digits[:, 2:3]
        chosen = jnp.where(key == last_parent * 8 + codes, 1.0, 0.0)
        spectrum = next_ref[r : r + 1, :total].astype(F32)
        a = jnp.sum(chosen * cc_ref[...], axis=0, keepdims=True) * spectrum
        b = jnp.sum(chosen * ss_ref[...], axis=0, keepdims=True) * spectrum
        add1 = a if add1 is None else add1 + a
        add2 = b if add2 is None else add2 + b
    g1_ref[parents - 1 : parents, :total] += add1
    g2_ref[parents - 1 : parents, :total] += add2
    real1, imag1 = split_halves(lambda k: g1_ref[:, k * LANES : (k + 1) * LANES], half)
    real2, imag2 = split_halves(lambda k: g2_ref[:, k * LANES : (k + 1) * LANES], half)
    for k in range(len(real1)):
        lhs_ref[:parents, k * LANES : (k + 1) * LANES] = (real1[k] + imag2[k]).astype(BF16)
        lhs_ref[parents:, k * LANES : (k + 1) * LANES] = (imag1[k] + real2[k]).astype(BF16)
    padded = len(real1) * LANES
    real, imag = [], []
    for start in range(0, padded, 256):
        width = min(256, half - start)
        p0 = jnp.dot(lhs_ref[:, :half], co_ref[0, :, start : start + width], preferred_element_type=F32)
        p1 = jnp.dot(lhs_ref[:, :half], co_ref[1, :, start : start + width], preferred_element_type=F32)
        g1_ref[:, start : start + width] = (p0[:parents] - p1[parents:]).astype(BF16).astype(F32)
        g2_ref[:, start : start + width] = (p1[:parents] + p0[parents:]).astype(BF16).astype(F32)
    for k in range(len(real1)):
        tile1 = g1_ref[:, k * LANES : (k + 1) * LANES]
        tile2 = g2_ref[:, k * LANES : (k + 1) * LANES]
        if k == len(real1) - 1:
            inside = lane_of(tile1.shape) < half - k * LANES
            tile1 = jnp.where(inside, tile1, 0.0)
            tile2 = jnp.where(inside, tile2, 0.0)
        real.append(tile1)
        imag.append(tile2)
        for g in range(parents // 8):
            row_ref[pl.ds(g * 128 + k, 8, stride=16), :] = tile1[g * 8 : g * 8 + 8]
            row_ref[pl.ds(g * 128 + 8 + k, 8, stride=16), :] = tile2[g * 8 : g * 8 + 8]

    def store(k, width, tile):
        up_ref[:, k * LANES : k * LANES + width] = tile.astype(BF16)

    join_halves(real, imag, half, store)
    rows_ref[...] = row_ref[...].reshape(parents, 16, LANES).astype(BF16)


VM = pl.BlockSpec(memory_space=pltpu.VMEM)
SM = pl.BlockSpec(memory_space=pltpu.SMEM)
HB = pl.BlockSpec(memory_space=pltpu.HBM)


def params(mib):
    return pltpu.CompilerParams(vmem_limit_bytes=mib << 20)


def cost(flops, nbytes):
    return pl.CostEstimate(flops=flops, bytes_accessed=nbytes, transcendentals=0)


def in_hbm(value):
    return pltpu.with_memory_space_constraint(value, pltpu.HBM)


def head_kernel(half, keys_hbm, leaf_hbm, head_ref, keys_ref, leaf_ref, sems):
    copies = [
        pltpu.make_async_copy(keys_hbm, keys_ref, sems.at[0]),
        pltpu.make_async_copy(leaf_hbm.at[:, 0:LANES], leaf_ref, sems.at[1]),
    ]
    for copy in copies:
        copy.start()
    total = 2 * half
    count = head_ref.shape[0]
    picker = jnp.where(
        lax.broadcasted_iota(jnp.int32, (16, LANES), 0) == lane_of((16, LANES)), 1.0, 0.0
    ).astype(BF16)
    copies[0].wait()
    for r in range(count):
        key = keys_ref[:, r : r + 1]
        for i, places in enumerate((16, 8, 0)):
            digit = lax.shift_right_logical(key, places) & 255
            head_ref[r : r + 1, total + i : total + i + 1] = digit.astype(F32).astype(BF16)
    copies[1].wait()
    head_ref[:, :total] = select_rows(picker, leaf_ref[...])[:count].astype(BF16)


def leaf_head(leaf_columns, keys_row):
    total = leaf_columns.shape[0]
    return pl.pallas_call(
        lambda *refs: head_kernel(total // 2, *refs),
        out_shape=pltpu.VMEM((2, total + 3), BF16),
        in_specs=[HB, HB],
        out_specs=VM,
        scratch_shapes=[
            pltpu.VMEM(keys_row.shape, jnp.int32),
            pltpu.VMEM((total, LANES), BF16),
            pltpu.SemaphoreType.DMA((2,)),
        ],
        compiler_params=params(2),
        name="leaf_head",
    )(in_hbm(keys_row), in_hbm(leaf_columns))


def gather_leaves(leaf_spectra, leaf_keys, parent_keys, child_phase, coarsen):
    half = child_phase.shape[1]
    leaves = leaf_spectra.shape[1]
    parents = parent_keys.shape[1]
    return pl.pallas_call(
        lambda *refs: gather_kernel(half, *refs),
        out_shape=(
            pltpu.VMEM((parents, 2048), F32),
            pltpu.VMEM((parents, 2048), F32),
            pltpu.VMEM((8, 2 * half), F32),
            pltpu.VMEM((8, 2 * half), F32),
            pltpu.VMEM(coarsen.shape, BF16),
        ),
        in_specs=[HB] * 5,
        out_specs=(VM, VM, VM, VM, VM),
        scratch_shapes=[
            pltpu.VMEM(leaf_keys.shape, jnp.int32),
            pltpu.VMEM(parent_keys.shape, jnp.int32),
            pltpu.VMEM((2 * half, leaves), BF16),
            pltpu.VMEM((8, half), F32),
            pltpu.SemaphoreType.DMA((5,)),
        ],
        compiler_params=params(12),
        cost_estimate=cost(8 << 28, 6 << 20),
        name="gather_leaves",
    )(*map(in_hbm, (leaf_keys, parent_keys, child_phase, leaf_spectra, coarsen)))


def upward_pass(parent_keys, following, cosines, sines, first, second, coarsen):
    half = coarsen.shape[1]
    parents = parent_keys.shape[1]
    return pl.pallas_call(
        lambda *refs: upward_kernel(half, *refs),
        out_shape=(
            jax.ShapeDtypeStruct((parents, 2 * half), BF16),
            pltpu.VMEM((parents, 16, LANES), BF16),
        ),
        in_specs=[VM] * 7,
        out_specs=(VM, VM),
        scratch_shapes=[
            pltpu.VMEM((parents, 2048), F32),
            pltpu.VMEM((parents, 2048), F32),
            pltpu.VMEM((2 * parents, 1024), BF16),
            pltpu.VMEM((parents * 16, LANES), F32),
        ],
        compiler_params=params(12),
        cost_estimate=cost(8 << 28, 6 << 20),
        name="upward_pass",
    )(parent_keys, following, cosines, sines, first, second, coarsen)


def coefficient_kernel(half, transfer_ref, after_ref, coef_ref, wide_ref):
    def lay_out(start, count):
        wide_ref[:count, : 2 * half] = transfer_ref[pl.ds(start, count), :].astype(F32)
        real, imag = split_halves(lambda k: wide_ref[:count, k * LANES : (k + 1) * LANES], half)
        for k in range(len(real)):
            for g in range(0, count, 8):
                size = min(8, count - g)
                coef_ref[pl.ds((start + g) * 16 + k, size, stride=16), :] = real[k][g : g + size]
                coef_ref[pl.ds((start + g) * 16 + 8 + k, size, stride=16), :] = imag[k][g : g + size]

    kinds = transfer_ref.shape[0]
    whole = kinds // 16

    def lay_out_step(i, _):
        lay_out(pl.multiple_of(i * 16, 16), 16)
        return 0

    lax.fori_loop(0, whole, lay_out_step, 0)
    if kinds % 16:
        lay_out(whole * 16, kinds % 16)


def coefficient_rows(transfer, after):
    kinds, width = transfer.shape
    return pl.pallas_call(
        lambda *refs: coefficient_kernel(width // 2, *refs),
        out_shape=pltpu.VMEM((kinds * 16, LANES), F32),
        in_specs=[VM, pl.BlockSpec(memory_space=pl.ANY)],
        out_specs=VM,
        scratch_shapes=[pltpu.VMEM((16, 2048), F32)],
        compiler_params=params(8),
        cost_estimate=cost(8 << 28, 6 << 20),
        name="coefficient_rows",
    )(transfer, after)


def table_kernel(*refs):
    block_refs, table_ref = refs[:HELD], refs[HELD]
    rows = block_refs[0].shape[0]
    odd = lax.rem(lax.axis_index("oct"), 2)
    for w in range(HELD):
        slot = w if w % 2 else w + 2 * odd * (1 - w)
        start = slot * (rows * 16)

        def widen(i, _, w=w, start=start):
            base = pl.multiple_of(start + i * 16, 16)
            table_ref[pl.ds(base, 16), :] = block_refs[w][i].astype(F32)
            return 0

        lax.fori_loop(0, rows, widen, 0, unroll=8)
    table_ref[HELD * rows * 16 : HELD * rows * 16 + 16, :] = jnp.zeros((16, LANES), F32)


def interact_kernel(first, groups, made, index_hbm, steps_hbm, *refs):
    count = 2 * UNROLL
    sems, live_ref, slot_refs = refs[-1], refs[-2], refs[-2 - count : -2]
    refs = refs[: -2 - count]
    per_target = ROW // UNROLL
    size = index_hbm.shape[0] // count
    live_copy = pltpu.make_async_copy(steps_hbm, live_ref, sems.at[len(groups), 0])
    live_copy.start()
    copies = []
    start = 0
    for g, targets in enumerate(groups):
        held, moved = start * per_target, targets * per_target
        copies.append([
            pltpu.make_async_copy(
                index_hbm.at[pl.ds(u * size + first * per_target + held, moved)],
                slot_refs[u].at[pl.ds(held, moved)],
                sems.at[g, u],
            )
            for u in range(count)
        ])
        for copy in copies[-1]:
            copy.start()
        start += targets
    if made:
        coef_ref, table_ref, out_ref = refs
    else:
        coef_ref, out_ref, table_ref = refs[HELD:]
        table_kernel(*refs[:HELD], table_ref)
    live_copy.wait()

    def one_target(j, _):
        base = j * per_target

        def some(at, chunks, sums):
            sums = list(sums)
            for c in range(chunks):
                for u in range(UNROLL):
                    s = pl.multiple_of(slot_refs[u][at + c], 16)
                    t = pl.multiple_of(slot_refs[UNROLL + u][at + c], 16)
                    sr = table_ref[pl.ds(s, 8), :]
                    si = table_ref[pl.ds(s + 8, 8), :]
                    cr = coef_ref[pl.ds(t, 8), :]
                    ci = coef_ref[pl.ds(t + 8, 8), :]
                    p = 2 * (u % 2)
                    sums[p] = sums[p] + (cr * sr - ci * si)
                    sums[p + 1] = sums[p + 1] + (cr * si + ci * sr)
            return tuple(sums)

        chunks = live_ref[first + j]
        pairs = lax.shift_right_logical(chunks, 1)
        sums = (jnp.zeros((8, LANES), F32),) * 4
        sums = lax.fori_loop(0, pairs, lambda i, c: some(base + 2 * i, 2, c), sums)
        sums = lax.fori_loop(0, chunks & 1, lambda i, c: some(base + 2 * pairs, 1, c), sums)
        out_ref[j, 0:8, :] = (sums[0] + sums[2]).astype(out_ref.dtype)
        out_ref[j, 8:16, :] = (sums[1] + sums[3]).astype(out_ref.dtype)
        return 0

    start = 0
    for g, targets in enumerate(groups):
        for copy in copies[g]:
            copy.wait()
        lax.fori_loop(start, start + targets, one_target, 0)
        start += targets


def interact(sources, index, steps, coefs, first, groups, dtype):
    made = not isinstance(sources, list)
    targets = sum(groups)
    out = pltpu.VMEM((targets, 16, LANES), dtype)
    operands = [coefs, sources] if made else [*sources, coefs]
    if not made:
        out = (out, pltpu.VMEM((HELD * sources[0].shape[0] * 16 + 16, LANES), F32))
    return pl.pallas_call(
        lambda *refs: interact_kernel(first, groups, made, *refs),
        out_shape=out,
        in_specs=[pl.BlockSpec(memory_space=pl.ANY)] * 2 + [VM] * len(operands),
        out_specs=VM if made else (VM, VM),
        scratch_shapes=[pltpu.SMEM((targets * (ROW // UNROLL),), jnp.int32)] * (2 * UNROLL)
        + [pltpu.SMEM(steps.shape, jnp.int32), pltpu.SemaphoreType.DMA((len(groups) + 1, 2 * UNROLL))],
        compiler_params=params(12),
        cost_estimate=cost(8 << 30, 6 << 20),
    )(index, steps, *operands)


def finish_kernel(half, near_ref, *refs):
    far_refs, out_ref, sum_ref = refs[:-2], refs[-2], refs[-1]
    targets = out_ref.shape[0]
    start = 0
    for far_ref in far_refs:
        count = far_ref.shape[0]
        sum_ref[start * 16 : (start + count) * 16, :] = (
            near_ref[start : start + count] + far_ref[...].astype(F32)
        ).reshape(count * 16, LANES)
        start += count
    count = -(-half // LANES)
    real, imag = [], []
    for k in range(count):
        real.append(jnp.concatenate([sum_ref[pl.ds(g * 128 + k, 8, stride=16), :] for g in range(targets // 8)], 0))
        imag.append(jnp.concatenate([sum_ref[pl.ds(g * 128 + 8 + k, 8, stride=16), :] for g in range(targets // 8)], 0))

    def store(k, width, tile):
        out_ref[:, k * LANES : k * LANES + width] = tile.astype(BF16)

    join_halves(real, imag, half, store)


def finish(near, fars, half):
    targets = near.shape[0]
    return pl.pallas_call(
        lambda *refs: finish_kernel(half, *refs),
        out_shape=jax.ShapeDtypeStruct((targets, 2 * half), BF16),
        in_specs=[VM] * (1 + len(fars)),
        out_specs=VM,
        scratch_shapes=[pltpu.VMEM((targets * 16, LANES), F32)],
        compiler_params=params(4),
        name="finish",
    )(near, *fars)


def shifted(value, distance):
    count = lax.axis_size("oct")
    return lax.ppermute(value, "oct", [(i, (i + distance) % count) for i in range(count)])


def shards(leaf_spectra, leaf_keys, parent_keys, child_phase, coarsen, transfer, vlist_src, vlist_type):
    count = lax.axis_size("oct")
    half = child_phase.shape[1]
    parents = parent_keys.shape[0]
    keys_row = leaf_keys.reshape(1, -1)
    parents_row = parent_keys.reshape(1, -1)
    leaf_columns = leaf_spectra.T
    head = leaf_head(leaf_columns, keys_row)
    following = lax.ppermute(head, "oct", [(i, i - 1) for i in range(1, count)])
    first, second, cosines, sines, coarsen = gather_leaves(leaf_columns, keys_row, parents_row, child_phase, coarsen)
    upward, rows = upward_pass(parents_row, following, cosines, sines, first, second, coarsen)

    behind2 = shifted(rows, 2)
    crossed = lax.ppermute(rows, "oct", [(i, (i + 1 + 2 * (i % 2)) % count) for i in range(count)])
    swapped = lax.ppermute(behind2, "oct", [(i, i ^ 1) for i in range(count)])
    blocks = [crossed, behind2, swapped, rows]

    packed = jnp.where(vlist_src < 0, DEAD, vlist_src * 512 + vlist_type)
    theirs = shifted(packed, -HELD)
    mine = jnp.where(vlist_src < 0, DEAD, (511 - vlist_src) * 512 + vlist_type)
    ordered = jnp.sort(jnp.concatenate([theirs, mine], 0), axis=1)
    ordered = jnp.pad(ordered, ((0, 0), (0, ROW - ordered.shape[1])), constant_values=DEAD)
    held = HELD * parents
    valid = ordered < held * 512
    steps = (jnp.sum(jnp.where(valid, 1, 0), axis=1).astype(jnp.int32) + (UNROLL - 1)) // UNROLL
    place = ordered >> 9
    is_mine = lax.broadcasted_iota(jnp.int32, place.shape, 0) >= parents
    place = jnp.where(is_mine, held - 1 - place, place)
    place = jnp.where(valid, place, held) * 16
    kind = jnp.where(valid, ordered & 511, 0) * 16

    def columns(table):
        return table.reshape(parents, ROW // UNROLL, UNROLL).transpose(2, 0, 1).reshape(-1)

    far_index = jnp.concatenate([columns(place[:parents]), columns(kind[:parents])])
    near_index = jnp.concatenate([columns(place[parents:]), columns(kind[parents:])])
    coefs = coefficient_rows(transfer, far_index)
    far_steps, near_steps = steps[:parents], steps[parents:]
    cut = parents // 2
    far1, table = interact(blocks, far_index, far_steps, coefs, 0, (8, cut - 8), BF16)
    arrived1 = shifted(far1, HELD)
    far2 = interact(table, far_index, far_steps, coefs, cut, (8, parents - cut - 8), BF16)
    arrived2 = shifted(far2, HELD)
    near = interact(table, near_index, near_steps, coefs, 0, (8, 24, parents - 32), F32)
    local_field = finish(near, [arrived1, arrived2], half)
    return upward, local_field


def solution(mesh):
    return jax.shard_map(
        shards,
        mesh=mesh,
        in_specs=(P("oct", None), P("oct"), P("oct"), P(), P(), P(), P("oct", None), P("oct", None)),
        out_specs=(P("oct", None), P("oct", None)),
        check_vma=False,
    )
```

```python
import jax
import jax.numpy as jnp
from jax import lax
from jax.experimental import pallas as pl
from jax.experimental.pallas import tpu as pltpu
from jax.sharding import PartitionSpec as P


F32 = jnp.float32
BF16 = jnp.bfloat16
LANES = 128
HELD = 4
SPLIT = 4
CHUNK = 16
ROW = 256
DEAD = 1 << 20


def lane_of(shape):
    return lax.broadcasted_iota(jnp.int32, shape, 1)


def split_halves(tile_of, half):
    count = -(-half // LANES)
    tail = half - (count - 1) * LANES
    shift = LANES - tail
    total = -(-2 * half // LANES)
    real, imag = [], []
    for k in range(count):
        tile = tile_of(k)
        if k == count - 1:
            tile = jnp.where(lane_of(tile.shape) < tail, tile, 0.0)
        real.append(tile)
        low = pltpu.roll(tile_of(count - 1 + k), shift, 1)
        if count + k < total:
            high = pltpu.roll(tile_of(count + k), shift, 1)
            low = jnp.where(lane_of(low.shape) < shift, low, high)
        if k == count - 1:
            low = jnp.where(lane_of(low.shape) < tail, low, 0.0)
        imag.append(low)
    return real, imag


def join_halves(real, imag, half, store):
    count = -(-half // LANES)
    tail = half - (count - 1) * LANES
    total = -(-2 * half // LANES)
    rolled = [pltpu.roll(tile, tail, 1) for tile in imag]
    for k in range(total):
        width = min(LANES, 2 * half - k * LANES)
        if k < count - 1:
            tile = real[k]
        elif k == count - 1:
            tile = jnp.where(lane_of(real[k].shape) < tail, real[k], rolled[0])
        else:
            j = k - count + 1
            tile = rolled[j - 1]
            if j < count:
                tile = jnp.where(lane_of(tile.shape) < tail, tile, rolled[j])
        store(k, width, tile[:, :width])


def select_rows(picker, columns):
    return lax.dot_general(picker, columns, (((1,), (1,)), ((), ())), preferred_element_type=F32)


def gather_kernel(half, keys_hbm, parents_hbm, phase_hbm, leaf_hbm,
                  g1_ref, g2_ref, cc_ref, ss_ref, keys_ref, parents_ref, leaf_ref, phase_ref, sems):
    copies = [
        pltpu.make_async_copy(src, dst, sems.at[i])
        for i, (src, dst) in enumerate((
            (keys_hbm, keys_ref), (parents_hbm, parents_ref), (phase_hbm, phase_ref),
            (leaf_hbm, leaf_ref),
        ))
    ]
    for copy in copies:
        copy.start()
    copies[0].wait()
    copies[1].wait()
    parents = parents_ref.shape[1]
    parent_row = jnp.broadcast_to(parents_ref[...].astype(F32), (parents, parents))
    diagonal = lax.broadcasted_iota(jnp.int32, (parents, parents), 0) == lane_of((parents, parents))
    parent_col = jnp.sum(jnp.where(diagonal, parent_row, 0.0), axis=1, keepdims=True).astype(jnp.int32)
    keys = keys_ref[...]
    picks = [
        jnp.where(keys == parent_col * 8 + code, 1.0, 0.0).astype(BF16) for code in range(8)
    ]
    picker = jnp.concatenate(picks, 0)
    copies[2].wait()
    cosine = jnp.cos(phase_ref[...])
    sine = jnp.sin(phase_ref[...])
    cc_ref[:, :half] = cosine
    cc_ref[:, half:] = cosine
    ss_ref[:, :half] = sine
    ss_ref[:, half:] = -sine
    copies[3].wait()
    total = 2 * half
    for start in range(0, total, 256):
        width = min(256, total - start)
        chosen = select_rows(picker, leaf_ref[start : start + width, :])
        first = second = None
        for code in range(8):
            part = chosen[code * parents : (code + 1) * parents]
            a = part * cc_ref[code : code + 1, start : start + width]
            b = part * ss_ref[code : code + 1, start : start + width]
            first = a if first is None else first + a
            second = b if second is None else second + b
        g1_ref[:, start : start + width] = first
        g2_ref[:, start : start + width] = second


def upward_kernel(half, parents_ref, next_ref, cc_ref, ss_ref, in1_ref, in2_ref, co_ref,
                  up_ref, rows_ref, g1_ref, g2_ref, lhs_ref, row_ref):
    parents = parents_ref.shape[1]
    total = 2 * half
    g1_ref[...] = in1_ref[...]
    g2_ref[...] = in2_ref[...]
    last_parent = parents_ref[:, parents - 1 : parents]
    add1 = add2 = None
    codes = lax.broadcasted_iota(jnp.int32, (8, 1), 0)
    for r in range(next_ref.shape[0]):
        digits = next_ref[r : r + 1, total : total + 3].astype(F32).astype(jnp.int32)
        key = digits[:, 0:1] * 65536 + digits[:, 1:2] * 256 + digits[:, 2:3]
        chosen = jnp.where(key == last_parent * 8 + codes, 1.0, 0.0)
        spectrum = next_ref[r : r + 1, :total].astype(F32)
        a = jnp.sum(chosen * cc_ref[...], axis=0, keepdims=True) * spectrum
        b = jnp.sum(chosen * ss_ref[...], axis=0, keepdims=True) * spectrum
        add1 = a if add1 is None else add1 + a
        add2 = b if add2 is None else add2 + b
    g1_ref[parents - 1 : parents, :total] += add1
    g2_ref[parents - 1 : parents, :total] += add2
    real1, imag1 = split_halves(lambda k: g1_ref[:, k * LANES : (k + 1) * LANES], half)
    real2, imag2 = split_halves(lambda k: g2_ref[:, k * LANES : (k + 1) * LANES], half)
    for k in range(len(real1)):
        lhs_ref[:parents, k * LANES : (k + 1) * LANES] = (real1[k] + imag2[k]).astype(BF16)
        lhs_ref[parents:, k * LANES : (k + 1) * LANES] = (imag1[k] + real2[k]).astype(BF16)
    padded = len(real1) * LANES
    real, imag = [], []
    for start in range(0, padded, 256):
        width = min(256, half - start)
        p0 = jnp.dot(lhs_ref[:, :half], co_ref[0, :, start : start + width], preferred_element_type=F32)
        p1 = jnp.dot(lhs_ref[:, :half], co_ref[1, :, start : start + width], preferred_element_type=F32)
        g1_ref[:, start : start + width] = (p0[:parents] - p1[parents:]).astype(BF16).astype(F32)
        g2_ref[:, start : start + width] = (p1[:parents] + p0[parents:]).astype(BF16).astype(F32)
    for k in range(len(real1)):
        tile1 = g1_ref[:, k * LANES : (k + 1) * LANES]
        tile2 = g2_ref[:, k * LANES : (k + 1) * LANES]
        if k == len(real1) - 1:
            inside = lane_of(tile1.shape) < half - k * LANES
            tile1 = jnp.where(inside, tile1, 0.0)
            tile2 = jnp.where(inside, tile2, 0.0)
        real.append(tile1)
        imag.append(tile2)
        for g in range(parents // 8):
            row_ref[pl.ds(g * 128 + k, 8, stride=16), :] = tile1[g * 8 : g * 8 + 8]
            row_ref[pl.ds(g * 128 + 8 + k, 8, stride=16), :] = tile2[g * 8 : g * 8 + 8]

    def store(k, width, tile):
        up_ref[:, k * LANES : k * LANES + width] = tile.astype(BF16)

    join_halves(real, imag, half, store)
    rows_ref[...] = row_ref[...].reshape(parents, 16, LANES).astype(BF16)


VM = pl.BlockSpec(memory_space=pltpu.VMEM)
SM = pl.BlockSpec(memory_space=pltpu.SMEM)
HB = pl.BlockSpec(memory_space=pltpu.HBM)


def params(mib):
    return pltpu.CompilerParams(vmem_limit_bytes=mib << 20)


def cost(flops, nbytes):
    return pl.CostEstimate(flops=flops, bytes_accessed=nbytes, transcendentals=0)


def in_hbm(value):
    return pltpu.with_memory_space_constraint(value, pltpu.HBM)


def head_kernel(half, keys_hbm, leaf_hbm, head_ref, keys_ref, leaf_ref, sems):
    copies = [
        pltpu.make_async_copy(keys_hbm, keys_ref, sems.at[0]),
        pltpu.make_async_copy(leaf_hbm.at[:, 0:LANES], leaf_ref, sems.at[1]),
    ]
    for copy in copies:
        copy.start()
    total = 2 * half
    count = head_ref.shape[0]
    picker = jnp.where(
        lax.broadcasted_iota(jnp.int32, (16, LANES), 0) == lane_of((16, LANES)), 1.0, 0.0
    ).astype(BF16)
    copies[0].wait()
    for r in range(count):
        key = keys_ref[:, r : r + 1]
        for i, places in enumerate((16, 8, 0)):
            digit = lax.shift_right_logical(key, places) & 255
            head_ref[r : r + 1, total + i : total + i + 1] = digit.astype(F32).astype(BF16)
    copies[1].wait()
    head_ref[:, :total] = select_rows(picker, leaf_ref[...])[:count].astype(BF16)


def leaf_head(leaf_columns, keys_row):
    total = leaf_columns.shape[0]
    return pl.pallas_call(
        lambda *refs: head_kernel(total // 2, *refs),
        out_shape=pltpu.VMEM((2, total + 3), BF16),
        in_specs=[HB, HB],
        out_specs=VM,
        scratch_shapes=[
            pltpu.VMEM(keys_row.shape, jnp.int32),
            pltpu.VMEM((total, LANES), BF16),
            pltpu.SemaphoreType.DMA((2,)),
        ],
        compiler_params=params(2),
        name="leaf_head",
    )(in_hbm(keys_row), in_hbm(leaf_columns))


def gather_leaves(leaf_spectra, leaf_keys, parent_keys, child_phase):
    half = child_phase.shape[1]
    leaves = leaf_spectra.shape[1]
    parents = parent_keys.shape[1]
    return pl.pallas_call(
        lambda *refs: gather_kernel(half, *refs),
        out_shape=(
            pltpu.VMEM((parents, 2048), F32),
            pltpu.VMEM((parents, 2048), F32),
            pltpu.VMEM((8, 2 * half), F32),
            pltpu.VMEM((8, 2 * half), F32),
        ),
        in_specs=[HB] * 4,
        out_specs=(VM, VM, VM, VM),
        scratch_shapes=[
            pltpu.VMEM(leaf_keys.shape, jnp.int32),
            pltpu.VMEM(parent_keys.shape, jnp.int32),
            pltpu.VMEM((2 * half, leaves), BF16),
            pltpu.VMEM((8, half), F32),
            pltpu.SemaphoreType.DMA((4,)),
        ],
        compiler_params=params(12),
        cost_estimate=cost(8 << 28, 6 << 20),
        name="gather_leaves",
    )(*map(in_hbm, (leaf_keys, parent_keys, child_phase, leaf_spectra)))


def upward_pass(parent_keys, following, cosines, sines, first, second, coarsen):
    half = coarsen.shape[1]
    parents = parent_keys.shape[1]
    return pl.pallas_call(
        lambda *refs: upward_kernel(half, *refs),
        out_shape=(
            jax.ShapeDtypeStruct((parents, 2 * half), BF16),
            pltpu.VMEM((parents, 16, LANES), BF16),
        ),
        in_specs=[VM] * 7,
        out_specs=(VM, VM),
        scratch_shapes=[
            pltpu.VMEM((parents, 2048), F32),
            pltpu.VMEM((parents, 2048), F32),
            pltpu.VMEM((2 * parents, 1024), BF16),
            pltpu.VMEM((parents * 16, LANES), F32),
        ],
        compiler_params=params(12),
        cost_estimate=cost(8 << 28, 6 << 20),
        name="upward_pass",
    )(parent_keys, following, cosines, sines, first, second, coarsen)


def coefficient_kernel(half, transfer_ref, after_ref, coef_ref, wide_ref):
    def lay_out(start, count):
        wide_ref[:count, : 2 * half] = transfer_ref[pl.ds(start, count), :].astype(F32)
        real, imag = split_halves(lambda k: wide_ref[:count, k * LANES : (k + 1) * LANES], half)
        for k in range(len(real)):
            for g in range(0, count, 8):
                size = min(8, count - g)
                coef_ref[pl.ds((start + g) * 16 + k, size, stride=16), :] = real[k][g : g + size]
                coef_ref[pl.ds((start + g) * 16 + 8 + k, size, stride=16), :] = imag[k][g : g + size]

    kinds = transfer_ref.shape[0]
    whole = kinds // 16

    def lay_out_step(i, _):
        lay_out(pl.multiple_of(i * 16, 16), 16)
        return 0

    lax.fori_loop(0, whole, lay_out_step, 0)
    if kinds % 16:
        lay_out(whole * 16, kinds % 16)


def coefficient_rows(transfer, after):
    kinds, width = transfer.shape
    return pl.pallas_call(
        lambda *refs: coefficient_kernel(width // 2, *refs),
        out_shape=pltpu.VMEM((kinds * 16, LANES), F32),
        in_specs=[VM, pl.BlockSpec(memory_space=pl.ANY)],
        out_specs=VM,
        scratch_shapes=[pltpu.VMEM((16, 2048), F32)],
        compiler_params=params(8),
        cost_estimate=cost(8 << 28, 6 << 20),
        name="coefficient_rows",
    )(transfer, after)


def table_kernel(*refs):
    block_refs, table_ref = refs[:HELD], refs[HELD]
    rows = block_refs[0].shape[0]
    odd = lax.rem(lax.axis_index("oct"), 2)
    for w in range(HELD):
        slot = w if w % 2 else w + 2 * odd * (1 - w)
        start = slot * (rows * 16)

        def widen(i, _, w=w, start=start):
            base = pl.multiple_of(start + i * 16, 16)
            table_ref[pl.ds(base, 16), :] = block_refs[w][i].astype(F32)
            return 0

        lax.fori_loop(0, rows, widen, 0, unroll=8)
    table_ref[HELD * rows * 16 : HELD * rows * 16 + 16, :] = jnp.zeros((16, LANES), F32)


def interact_kernel(first, groups, made, index_hbm, steps_hbm, *refs):
    count = 2 * SPLIT
    sems, live_ref, slot_refs = refs[-1], refs[-2], refs[-2 - count : -2]
    refs = refs[: -2 - count]
    per_target = ROW // SPLIT
    size = index_hbm.shape[0] // count
    live_copy = pltpu.make_async_copy(steps_hbm, live_ref, sems.at[len(groups), 0])
    live_copy.start()
    copies = []
    start = 0
    for g, targets in enumerate(groups):
        held, moved = start * per_target, targets * per_target
        copies.append([
            pltpu.make_async_copy(
                index_hbm.at[pl.ds(u * size + first * per_target + held, moved)],
                slot_refs[u].at[pl.ds(held, moved)],
                sems.at[g, u],
            )
            for u in range(count)
        ])
        start += targets
    for copy in copies[0]:
        copy.start()
    if made:
        coef_ref, table_ref, out_ref = refs
    else:
        coef_ref, out_ref, table_ref = refs[HELD:]
        table_kernel(*refs[:HELD], table_ref)
    live_copy.wait()

    def one_target(j, _):
        base = j * per_target

        def some(at, slots, sums):
            sums = list(sums)
            for c in range(slots // SPLIT):
                for u in range(SPLIT):
                    s = pl.multiple_of(slot_refs[u][at + c], 16)
                    t = pl.multiple_of(slot_refs[SPLIT + u][at + c], 16)
                    sr = table_ref[pl.ds(s, 8), :]
                    si = table_ref[pl.ds(s + 8, 8), :]
                    cr = coef_ref[pl.ds(t, 8), :]
                    ci = coef_ref[pl.ds(t + 8, 8), :]
                    p = 2 * (u % 2)
                    sums[p] = sums[p] + (cr * sr - ci * si)
                    sums[p + 1] = sums[p + 1] + (cr * si + ci * sr)
            return tuple(sums)

        chunks = live_ref[first + j]
        pairs = lax.shift_right_logical(chunks, 1)
        sums = (jnp.zeros((8, LANES), F32),) * 4
        width = 2 * CHUNK // SPLIT
        sums = lax.fori_loop(0, pairs, lambda i, c: some(base + width * i, 2 * CHUNK, c), sums)
        sums = lax.fori_loop(0, chunks & 1, lambda i, c: some(base + width * pairs, CHUNK, c), sums)
        out_ref[j, 0:8, :] = (sums[0] + sums[2]).astype(out_ref.dtype)
        out_ref[j, 8:16, :] = (sums[1] + sums[3]).astype(out_ref.dtype)
        return 0

    start = 0
    for g, targets in enumerate(groups):
        for copy in copies[g]:
            copy.wait()
        if g + 1 < len(groups):
            for copy in copies[g + 1]:
                copy.start()
        lax.fori_loop(start, start + targets, one_target, 0)
        start += targets


def interact(sources, index, steps, coefs, first, groups, dtype):
    made = not isinstance(sources, list)
    targets = sum(groups)
    out = pltpu.VMEM((targets, 16, LANES), dtype)
    operands = [coefs, sources] if made else [*sources, coefs]
    if not made:
        out = (out, pltpu.VMEM((HELD * sources[0].shape[0] * 16 + 16, LANES), F32))
    return pl.pallas_call(
        lambda *refs: interact_kernel(first, groups, made, *refs),
        out_shape=out,
        in_specs=[pl.BlockSpec(memory_space=pl.ANY)] * 2 + [VM] * len(operands),
        out_specs=VM if made else (VM, VM),
        scratch_shapes=[pltpu.SMEM((targets * (ROW // SPLIT),), jnp.int32)] * (2 * SPLIT)
        + [pltpu.SMEM(steps.shape, jnp.int32), pltpu.SemaphoreType.DMA((len(groups) + 1, 2 * SPLIT))],
        compiler_params=params(12),
        cost_estimate=cost(8 << 30, 6 << 20),
    )(index, steps, *operands)


def finish_kernel(half, near_ref, *refs):
    far_refs, out_ref, sum_ref = refs[:-2], refs[-2], refs[-1]
    targets = out_ref.shape[0]
    start = 0
    for far_ref in far_refs:
        count = far_ref.shape[0]
        sum_ref[start * 16 : (start + count) * 16, :] = (
            near_ref[start : start + count] + far_ref[...].astype(F32)
        ).reshape(count * 16, LANES)
        start += count
    count = -(-half // LANES)
    real, imag = [], []
    for k in range(count):
        real.append(jnp.concatenate([sum_ref[pl.ds(g * 128 + k, 8, stride=16), :] for g in range(targets // 8)], 0))
        imag.append(jnp.concatenate([sum_ref[pl.ds(g * 128 + 8 + k, 8, stride=16), :] for g in range(targets // 8)], 0))

    def store(k, width, tile):
        out_ref[:, k * LANES : k * LANES + width] = tile.astype(BF16)

    join_halves(real, imag, half, store)


def finish(near, fars, half):
    targets = near.shape[0]
    return pl.pallas_call(
        lambda *refs: finish_kernel(half, *refs),
        out_shape=jax.ShapeDtypeStruct((targets, 2 * half), BF16),
        in_specs=[VM] * (1 + len(fars)),
        out_specs=VM,
        scratch_shapes=[pltpu.VMEM((targets * 16, LANES), F32)],
        compiler_params=params(4),
        name="finish",
    )(near, *fars)


def shifted(value, distance):
    count = lax.axis_size("oct")
    return lax.ppermute(value, "oct", [(i, (i + distance) % count) for i in range(count)])


def shards(leaf_spectra, leaf_keys, parent_keys, child_phase, coarsen, transfer, vlist_src, vlist_type):
    count = lax.axis_size("oct")
    half = child_phase.shape[1]
    parents = parent_keys.shape[0]
    keys_row = leaf_keys.reshape(1, -1)
    parents_row = parent_keys.reshape(1, -1)
    leaf_columns = leaf_spectra.T
    head = leaf_head(leaf_columns, keys_row)
    following = lax.ppermute(head, "oct", [(i, i - 1) for i in range(1, count)])
    first, second, cosines, sines = gather_leaves(leaf_columns, keys_row, parents_row, child_phase)
    upward, rows = upward_pass(parents_row, following, cosines, sines, first, second, coarsen)

    behind2 = shifted(rows, 2)
    crossed = lax.ppermute(rows, "oct", [(i, (i + 1 + 2 * (i % 2)) % count) for i in range(count)])
    swapped = lax.ppermute(behind2, "oct", [(i, i ^ 1) for i in range(count)])
    blocks = [crossed, behind2, swapped, rows]

    vlist_src, vlist_type, _ = lax.optimization_barrier((vlist_src, vlist_type, upward))
    packed = jnp.where(vlist_src < 0, DEAD, vlist_src * 512 + vlist_type)
    theirs = shifted(packed, -HELD)
    mine = jnp.where(vlist_src < 0, DEAD, (511 - vlist_src) * 512 + vlist_type)
    ordered = jnp.sort(jnp.concatenate([theirs, mine], 0), axis=1)
    ordered = jnp.pad(ordered, ((0, 0), (0, ROW - ordered.shape[1])), constant_values=DEAD)
    held = HELD * parents
    valid = ordered < held * 512
    steps = (jnp.sum(jnp.where(valid, 1, 0), axis=1).astype(jnp.int32) + (CHUNK - 1)) // CHUNK
    place = ordered >> 9
    is_mine = lax.broadcasted_iota(jnp.int32, place.shape, 0) >= parents
    place = jnp.where(is_mine, held - 1 - place, place)
    place = jnp.where(valid, place, held) * 16
    kind = jnp.where(valid, ordered & 511, 0) * 16

    def columns(table):
        return table.reshape(parents, ROW // SPLIT, SPLIT).transpose(2, 0, 1).reshape(-1)

    far_index = jnp.concatenate([columns(place[:parents]), columns(kind[:parents])])
    near_index = jnp.concatenate([columns(place[parents:]), columns(kind[parents:])])
    coefs = coefficient_rows(transfer, far_index)
    far_steps, near_steps = steps[:parents], steps[parents:]
    cut = 5 * parents // 8
    far1, table = interact(blocks, far_index, far_steps, coefs, 0, (8, 16, cut - 24), BF16)
    arrived1 = shifted(far1, HELD)
    far2 = interact(table, far_index, far_steps, coefs, cut, (8, parents - cut - 8), BF16)
    arrived2 = shifted(far2, HELD)
    near = interact(table, near_index, near_steps, coefs, 0, (8, 16, parents - 24), F32)
    local_field = finish(near, [arrived1, arrived2], half)
    return upward, local_field


def solution(mesh):
    return jax.shard_map(
        shards,
        mesh=mesh,
        in_specs=(P("oct", None), P("oct"), P("oct"), P(), P(), P(), P("oct", None), P("oct", None)),
        out_specs=(P("oct", None), P("oct", None)),
        check_vma=False,
    )
```

```python
import jax
import jax.numpy as jnp
from jax import lax
from jax.experimental import pallas as pl
from jax.experimental.pallas import tpu as pltpu
from jax.sharding import PartitionSpec as P


F32 = jnp.float32
BF16 = jnp.bfloat16
LANES = 128
HELD = 4
SPLIT = 4
CHUNK = 16
ROW = 256
DEAD = 1 << 20


def lane_of(shape):
    return lax.broadcasted_iota(jnp.int32, shape, 1)


def split_halves(tile_of, half):
    count = -(-half // LANES)
    tail = half - (count - 1) * LANES
    shift = LANES - tail
    total = -(-2 * half // LANES)
    real, imag = [], []
    for k in range(count):
        tile = tile_of(k)
        if k == count - 1:
            tile = jnp.where(lane_of(tile.shape) < tail, tile, 0.0)
        real.append(tile)
        low = pltpu.roll(tile_of(count - 1 + k), shift, 1)
        if count + k < total:
            high = pltpu.roll(tile_of(count + k), shift, 1)
            low = jnp.where(lane_of(low.shape) < shift, low, high)
        if k == count - 1:
            low = jnp.where(lane_of(low.shape) < tail, low, 0.0)
        imag.append(low)
    return real, imag


def join_halves(real, imag, half, store):
    count = -(-half // LANES)
    tail = half - (count - 1) * LANES
    total = -(-2 * half // LANES)
    rolled = [pltpu.roll(tile, tail, 1) for tile in imag]
    for k in range(total):
        width = min(LANES, 2 * half - k * LANES)
        if k < count - 1:
            tile = real[k]
        elif k == count - 1:
            tile = jnp.where(lane_of(real[k].shape) < tail, real[k], rolled[0])
        else:
            j = k - count + 1
            tile = rolled[j - 1]
            if j < count:
                tile = jnp.where(lane_of(tile.shape) < tail, tile, rolled[j])
        store(k, width, tile[:, :width])


def select_rows(picker, columns):
    return lax.dot_general(picker, columns, (((1,), (1,)), ((), ())), preferred_element_type=F32)


def gather_kernel(half, keys_ref, parents_ref, phase_ref, leaf_ref, coarsen_hbm,
                  g1_ref, g2_ref, cc_ref, ss_ref, co_ref, sem):
    copy = pltpu.make_async_copy(coarsen_hbm.at[0], co_ref, sem)
    copy.start()
    parents = parents_ref.shape[1]
    parent_row = jnp.broadcast_to(parents_ref[...].astype(F32), (parents, parents))
    diagonal = lax.broadcasted_iota(jnp.int32, (parents, parents), 0) == lane_of((parents, parents))
    parent_col = jnp.sum(jnp.where(diagonal, parent_row, 0.0), axis=1, keepdims=True).astype(jnp.int32)
    keys = keys_ref[...]
    picks = [
        jnp.where(keys == parent_col * 8 + code, 1.0, 0.0).astype(BF16) for code in range(8)
    ]
    picker = jnp.concatenate(picks, 0)
    cosine = jnp.cos(phase_ref[...])
    sine = jnp.sin(phase_ref[...])
    cc_ref[:, :half] = cosine
    cc_ref[:, half:] = cosine
    ss_ref[:, :half] = sine
    ss_ref[:, half:] = -sine
    total = 2 * half
    for start in range(0, total, 256):
        width = min(256, total - start)
        chosen = select_rows(picker, leaf_ref[start : start + width, :])
        first = second = None
        for code in range(8):
            part = chosen[code * parents : (code + 1) * parents]
            a = part * cc_ref[code : code + 1, start : start + width]
            b = part * ss_ref[code : code + 1, start : start + width]
            first = a if first is None else first + a
            second = b if second is None else second + b
        g1_ref[:, start : start + width] = first
        g2_ref[:, start : start + width] = second
    copy.wait()


def upward_kernel(half, parents_ref, next_ref, cc_ref, ss_ref, in1_ref, in2_ref, co_ref, coarsen_hbm,
                  up_ref, rows_ref, g1_ref, g2_ref, lhs_ref, row_ref, co_imag_ref, sem):
    copy = pltpu.make_async_copy(coarsen_hbm.at[1], co_imag_ref, sem)
    copy.start()
    parents = parents_ref.shape[1]
    total = 2 * half
    g1_ref[...] = in1_ref[...]
    g2_ref[...] = in2_ref[...]
    last_parent = parents_ref[:, parents - 1 : parents]
    add1 = add2 = None
    codes = lax.broadcasted_iota(jnp.int32, (8, 1), 0)
    for r in range(next_ref.shape[0]):
        digits = next_ref[r : r + 1, total : total + 3].astype(F32).astype(jnp.int32)
        key = digits[:, 0:1] * 65536 + digits[:, 1:2] * 256 + digits[:, 2:3]
        chosen = jnp.where(key == last_parent * 8 + codes, 1.0, 0.0)
        spectrum = next_ref[r : r + 1, :total].astype(F32)
        a = jnp.sum(chosen * cc_ref[...], axis=0, keepdims=True) * spectrum
        b = jnp.sum(chosen * ss_ref[...], axis=0, keepdims=True) * spectrum
        add1 = a if add1 is None else add1 + a
        add2 = b if add2 is None else add2 + b
    g1_ref[parents - 1 : parents, :total] += add1
    g2_ref[parents - 1 : parents, :total] += add2
    real1, imag1 = split_halves(lambda k: g1_ref[:, k * LANES : (k + 1) * LANES], half)
    real2, imag2 = split_halves(lambda k: g2_ref[:, k * LANES : (k + 1) * LANES], half)
    for k in range(len(real1)):
        lhs_ref[:parents, k * LANES : (k + 1) * LANES] = (real1[k] + imag2[k]).astype(BF16)
        lhs_ref[parents:, k * LANES : (k + 1) * LANES] = (imag1[k] + real2[k]).astype(BF16)
    copy.wait()
    padded = len(real1) * LANES
    real, imag = [], []
    for start in range(0, padded, 256):
        width = min(256, half - start)
        p0 = jnp.dot(lhs_ref[:, :half], co_ref[:, start : start + width], preferred_element_type=F32)
        p1 = jnp.dot(lhs_ref[:, :half], co_imag_ref[:, start : start + width], preferred_element_type=F32)
        g1_ref[:, start : start + width] = (p0[:parents] - p1[parents:]).astype(BF16).astype(F32)
        g2_ref[:, start : start + width] = (p1[:parents] + p0[parents:]).astype(BF16).astype(F32)
    for k in range(len(real1)):
        tile1 = g1_ref[:, k * LANES : (k + 1) * LANES]
        tile2 = g2_ref[:, k * LANES : (k + 1) * LANES]
        if k == len(real1) - 1:
            inside = lane_of(tile1.shape) < half - k * LANES
            tile1 = jnp.where(inside, tile1, 0.0)
            tile2 = jnp.where(inside, tile2, 0.0)
        real.append(tile1)
        imag.append(tile2)
        for g in range(parents // 8):
            row_ref[pl.ds(g * 128 + k, 8, stride=16), :] = tile1[g * 8 : g * 8 + 8]
            row_ref[pl.ds(g * 128 + 8 + k, 8, stride=16), :] = tile2[g * 8 : g * 8 + 8]

    def store(k, width, tile):
        up_ref[:, k * LANES : k * LANES + width] = tile.astype(BF16)

    join_halves(real, imag, half, store)
    rows_ref[...] = row_ref[...].reshape(parents, 16, LANES).astype(BF16)


VM = pl.BlockSpec(memory_space=pltpu.VMEM)
SM = pl.BlockSpec(memory_space=pltpu.SMEM)
HB = pl.BlockSpec(memory_space=pltpu.HBM)


def params(mib):
    return pltpu.CompilerParams(vmem_limit_bytes=mib << 20)


def cost(flops, nbytes):
    return pl.CostEstimate(flops=flops, bytes_accessed=nbytes, transcendentals=0)


def in_hbm(value):
    return pltpu.with_memory_space_constraint(value, pltpu.HBM)


def head_kernel(half, keys_hbm, parents_hbm, phase_hbm, leaf_hbm,
                head_ref, keys_ref, parents_ref, phase_ref, leaf_ref, sems):
    copies = [
        pltpu.make_async_copy(src, dst, sems.at[i])
        for i, (src, dst) in enumerate((
            (leaf_hbm, leaf_ref), (keys_hbm, keys_ref), (parents_hbm, parents_ref), (phase_hbm, phase_ref),
        ))
    ]
    for copy in copies:
        copy.start()
    total = 2 * half
    count = head_ref.shape[0]
    picker = jnp.where(
        lax.broadcasted_iota(jnp.int32, (16, LANES), 0) == lane_of((16, LANES)), 1.0, 0.0
    ).astype(BF16)
    copies[1].wait()
    for r in range(count):
        key = keys_ref[:, r : r + 1]
        for i, places in enumerate((16, 8, 0)):
            digit = lax.shift_right_logical(key, places) & 255
            head_ref[r : r + 1, total + i : total + i + 1] = digit.astype(F32).astype(BF16)
    copies[2].wait()
    copies[3].wait()
    copies[0].wait()
    head_ref[:, :total] = select_rows(picker, leaf_ref[:, 0:LANES])[:count].astype(BF16)


def leaf_head(keys_row, parents_row, child_phase, leaf_columns):
    total = leaf_columns.shape[0]
    operands = (keys_row, parents_row, child_phase, leaf_columns)
    return pl.pallas_call(
        lambda *refs: head_kernel(total // 2, *refs),
        out_shape=(pltpu.VMEM((2, total + 3), BF16), *(pltpu.VMEM(x.shape, x.dtype) for x in operands)),
        in_specs=[HB] * 4,
        out_specs=(VM,) * 5,
        scratch_shapes=[pltpu.SemaphoreType.DMA((4,))],
        compiler_params=params(4),
        name="leaf_head",
    )(*map(in_hbm, operands))


def gather_leaves(leaf_spectra, leaf_keys, parent_keys, child_phase, coarsen):
    half = child_phase.shape[1]
    parents = parent_keys.shape[1]
    return pl.pallas_call(
        lambda *refs: gather_kernel(half, *refs),
        out_shape=(
            pltpu.VMEM((parents, 2048), F32),
            pltpu.VMEM((parents, 2048), F32),
            pltpu.VMEM((8, 2 * half), F32),
            pltpu.VMEM((8, 2 * half), F32),
            pltpu.VMEM((half, half), BF16),
        ),
        in_specs=[VM] * 4 + [HB],
        out_specs=(VM,) * 5,
        scratch_shapes=[pltpu.SemaphoreType.DMA],
        compiler_params=params(12),
        cost_estimate=cost(8 << 28, 6 << 20),
        name="gather_leaves",
    )(leaf_keys, parent_keys, child_phase, leaf_spectra, in_hbm(coarsen))


def upward_pass(parent_keys, following, cosines, sines, first, second, coarsen_real, coarsen):
    half = coarsen.shape[1]
    parents = parent_keys.shape[1]
    return pl.pallas_call(
        lambda *refs: upward_kernel(half, *refs),
        out_shape=(
            jax.ShapeDtypeStruct((parents, 2 * half), BF16),
            pltpu.VMEM((parents, 16, LANES), BF16),
        ),
        in_specs=[VM] * 7 + [HB],
        out_specs=(VM, VM),
        scratch_shapes=[
            pltpu.VMEM((parents, 2048), F32),
            pltpu.VMEM((parents, 2048), F32),
            pltpu.VMEM((2 * parents, 1024), BF16),
            pltpu.VMEM((parents * 16, LANES), F32),
            pltpu.VMEM((half, half), BF16),
            pltpu.SemaphoreType.DMA,
        ],
        compiler_params=params(12),
        cost_estimate=cost(8 << 28, 6 << 20),
        name="upward_pass",
    )(parent_keys, following, cosines, sines, first, second, coarsen_real, in_hbm(coarsen))


def coefficient_kernel(half, transfer_ref, after_ref, coef_ref, wide_ref):
    def lay_out(start, count):
        wide_ref[:count, : 2 * half] = transfer_ref[pl.ds(start, count), :].astype(F32)
        real, imag = split_halves(lambda k: wide_ref[:count, k * LANES : (k + 1) * LANES], half)
        for k in range(len(real)):
            for g in range(0, count, 8):
                size = min(8, count - g)
                coef_ref[pl.ds((start + g) * 16 + k, size, stride=16), :] = real[k][g : g + size]
                coef_ref[pl.ds((start + g) * 16 + 8 + k, size, stride=16), :] = imag[k][g : g + size]

    kinds = transfer_ref.shape[0]
    whole = kinds // 16

    def lay_out_step(i, _):
        lay_out(pl.multiple_of(i * 16, 16), 16)
        return 0

    lax.fori_loop(0, whole, lay_out_step, 0)
    if kinds % 16:
        lay_out(whole * 16, kinds % 16)


def coefficient_rows(transfer, after):
    kinds, width = transfer.shape
    return pl.pallas_call(
        lambda *refs: coefficient_kernel(width // 2, *refs),
        out_shape=pltpu.VMEM((kinds * 16, LANES), F32),
        in_specs=[VM, pl.BlockSpec(memory_space=pl.ANY)],
        out_specs=VM,
        scratch_shapes=[pltpu.VMEM((16, 2048), F32)],
        compiler_params=params(8),
        cost_estimate=cost(8 << 28, 6 << 20),
        name="coefficient_rows",
    )(transfer, after)


def table_kernel(*refs):
    block_refs, table_ref = refs[:HELD], refs[HELD]
    rows = block_refs[0].shape[0]
    odd = lax.rem(lax.axis_index("oct"), 2)
    for w in range(HELD):
        slot = w if w % 2 else w + 2 * odd * (1 - w)
        start = slot * (rows * 16)

        def widen(i, _, w=w, start=start):
            base = pl.multiple_of(start + i * 16, 16)
            table_ref[pl.ds(base, 16), :] = block_refs[w][i].astype(F32)
            return 0

        lax.fori_loop(0, rows, widen, 0, unroll=8)
    table_ref[HELD * rows * 16 : HELD * rows * 16 + 16, :] = jnp.zeros((16, LANES), F32)


def interact_kernel(first, groups, made, index_hbm, steps_hbm, *refs):
    count = 2 * SPLIT
    sems, live_ref, slot_refs = refs[-1], refs[-2], refs[-2 - count : -2]
    refs = refs[: -2 - count]
    per_target = ROW // SPLIT
    size = index_hbm.shape[0] // count
    live_copy = pltpu.make_async_copy(steps_hbm, live_ref, sems.at[len(groups), 0])
    live_copy.start()
    copies = []
    start = 0
    for g, targets in enumerate(groups):
        held, moved = start * per_target, targets * per_target
        copies.append([
            pltpu.make_async_copy(
                index_hbm.at[pl.ds(u * size + first * per_target + held, moved)],
                slot_refs[u].at[pl.ds(held, moved)],
                sems.at[g, u],
            )
            for u in range(count)
        ])
        start += targets
    for copy in copies[0]:
        copy.start()
    if made:
        coef_ref, table_ref, out_ref = refs
    else:
        coef_ref, out_ref, table_ref = refs[HELD:]
        table_kernel(*refs[:HELD], table_ref)
    live_copy.wait()

    def one_target(j, _):
        base = j * per_target

        def some(at, slots, sums):
            sums = list(sums)
            for c in range(slots // SPLIT):
                for u in range(SPLIT):
                    s = pl.multiple_of(slot_refs[u][at + c], 16)
                    t = pl.multiple_of(slot_refs[SPLIT + u][at + c], 16)
                    sr = table_ref[pl.ds(s, 8), :]
                    si = table_ref[pl.ds(s + 8, 8), :]
                    cr = coef_ref[pl.ds(t, 8), :]
                    ci = coef_ref[pl.ds(t + 8, 8), :]
                    p = 2 * (u % 2)
                    sums[p] = sums[p] + (cr * sr - ci * si)
                    sums[p + 1] = sums[p + 1] + (cr * si + ci * sr)
            return tuple(sums)

        chunks = live_ref[first + j]
        pairs = lax.shift_right_logical(chunks, 1)
        sums = (jnp.zeros((8, LANES), F32),) * 4
        width = 2 * CHUNK // SPLIT
        sums = lax.fori_loop(0, pairs, lambda i, c: some(base + width * i, 2 * CHUNK, c), sums)
        sums = lax.fori_loop(0, chunks & 1, lambda i, c: some(base + width * pairs, CHUNK, c), sums)
        out_ref[j, 0:8, :] = (sums[0] + sums[2]).astype(out_ref.dtype)
        out_ref[j, 8:16, :] = (sums[1] + sums[3]).astype(out_ref.dtype)
        return 0

    start = 0
    for g, targets in enumerate(groups):
        for copy in copies[g]:
            copy.wait()
        if g + 1 < len(groups):
            for copy in copies[g + 1]:
                copy.start()
        lax.fori_loop(start, start + targets, one_target, 0)
        start += targets


def interact(sources, index, steps, coefs, first, groups, dtype):
    made = not isinstance(sources, list)
    targets = sum(groups)
    out = pltpu.VMEM((targets, 16, LANES), dtype)
    operands = [coefs, sources] if made else [*sources, coefs]
    if not made:
        out = (out, pltpu.VMEM((HELD * sources[0].shape[0] * 16 + 16, LANES), F32))
    return pl.pallas_call(
        lambda *refs: interact_kernel(first, groups, made, *refs),
        out_shape=out,
        in_specs=[pl.BlockSpec(memory_space=pl.ANY)] * 2 + [VM] * len(operands),
        out_specs=VM if made else (VM, VM),
        scratch_shapes=[pltpu.SMEM((targets * (ROW // SPLIT),), jnp.int32)] * (2 * SPLIT)
        + [pltpu.SMEM(steps.shape, jnp.int32), pltpu.SemaphoreType.DMA((len(groups) + 1, 2 * SPLIT))],
        compiler_params=params(12),
        cost_estimate=cost(8 << 30, 6 << 20),
    )(index, steps, *operands)


def finish_kernel(half, near_ref, *refs):
    far_refs, out_ref, sum_ref = refs[:-2], refs[-2], refs[-1]
    targets = out_ref.shape[0]
    start = 0
    for far_ref in far_refs:
        count = far_ref.shape[0]
        sum_ref[start * 16 : (start + count) * 16, :] = (
            near_ref[start : start + count] + far_ref[...].astype(F32)
        ).reshape(count * 16, LANES)
        start += count
    count = -(-half // LANES)
    real, imag = [], []
    for k in range(count):
        real.append(jnp.concatenate([sum_ref[pl.ds(g * 128 + k, 8, stride=16), :] for g in range(targets // 8)], 0))
        imag.append(jnp.concatenate([sum_ref[pl.ds(g * 128 + 8 + k, 8, stride=16), :] for g in range(targets // 8)], 0))

    def store(k, width, tile):
        out_ref[:, k * LANES : k * LANES + width] = tile.astype(BF16)

    join_halves(real, imag, half, store)


def finish(near, fars, half):
    targets = near.shape[0]
    return pl.pallas_call(
        lambda *refs: finish_kernel(half, *refs),
        out_shape=jax.ShapeDtypeStruct((targets, 2 * half), BF16),
        in_specs=[VM] * (1 + len(fars)),
        out_specs=VM,
        scratch_shapes=[pltpu.VMEM((targets * 16, LANES), F32)],
        compiler_params=params(4),
        name="finish",
    )(near, *fars)


def shifted(value, distance):
    count = lax.axis_size("oct")
    return lax.ppermute(value, "oct", [(i, (i + distance) % count) for i in range(count)])


def shards(leaf_spectra, leaf_keys, parent_keys, child_phase, coarsen, transfer, vlist_src, vlist_type):
    count = lax.axis_size("oct")
    half = child_phase.shape[1]
    parents = parent_keys.shape[0]
    keys_row = leaf_keys.reshape(1, -1)
    parents_row = parent_keys.reshape(1, -1)
    leaf_columns = leaf_spectra.T
    head, keys_row, parents_row, child_phase, leaf_columns = leaf_head(
        keys_row, parents_row, child_phase, leaf_columns
    )
    following = lax.ppermute(head, "oct", [(i, i - 1) for i in range(1, count)])
    first, second, cosines, sines, coarsen_real = gather_leaves(
        leaf_columns, keys_row, parents_row, child_phase, coarsen
    )
    upward, rows = upward_pass(parents_row, following, cosines, sines, first, second, coarsen_real, coarsen)

    behind2 = shifted(rows, 2)
    crossed = lax.ppermute(rows, "oct", [(i, (i + 1 + 2 * (i % 2)) % count) for i in range(count)])
    swapped = lax.ppermute(behind2, "oct", [(i, i ^ 1) for i in range(count)])
    blocks = [crossed, behind2, swapped, rows]

    vlist_src, vlist_type, _ = lax.optimization_barrier((vlist_src, vlist_type, upward))
    packed = jnp.where(vlist_src < 0, DEAD, vlist_src * 512 + vlist_type)
    theirs = shifted(packed, -HELD)
    mine = jnp.where(vlist_src < 0, DEAD, (511 - vlist_src) * 512 + vlist_type)
    ordered = jnp.sort(jnp.concatenate([theirs, mine], 0), axis=1)
    ordered = jnp.pad(ordered, ((0, 0), (0, ROW - ordered.shape[1])), constant_values=DEAD)
    held = HELD * parents
    valid = ordered < held * 512
    steps = (jnp.sum(jnp.where(valid, 1, 0), axis=1).astype(jnp.int32) + (CHUNK - 1)) // CHUNK
    place = ordered >> 9
    is_mine = lax.broadcasted_iota(jnp.int32, place.shape, 0) >= parents
    place = jnp.where(is_mine, held - 1 - place, place)
    place = jnp.where(valid, place, held) * 16
    kind = jnp.where(valid, ordered & 511, 0) * 16

    def columns(table):
        return table.reshape(parents, ROW // SPLIT, SPLIT).transpose(2, 0, 1).reshape(-1)

    far_index = jnp.concatenate([columns(place[:parents]), columns(kind[:parents])])
    near_index = jnp.concatenate([columns(place[parents:]), columns(kind[parents:])])
    coefs = coefficient_rows(transfer, far_index)
    far_steps, near_steps = steps[:parents], steps[parents:]
    cut = 5 * parents // 8
    far1, table = interact(blocks, far_index, far_steps, coefs, 0, (8, 16, cut - 24), BF16)
    arrived1 = shifted(far1, HELD)
    far2 = interact(table, far_index, far_steps, coefs, cut, (8, parents - cut - 8), BF16)
    arrived2 = shifted(far2, HELD)
    near = interact(table, near_index, near_steps, coefs, 0, (8, 16, parents - 24), F32)
    local_field = finish(near, [arrived1, arrived2], half)
    return upward, local_field


def solution(mesh):
    return jax.shard_map(
        shards,
        mesh=mesh,
        in_specs=(P("oct", None), P("oct"), P("oct"), P(), P(), P(), P("oct", None), P("oct", None)),
        out_specs=(P("oct", None), P("oct", None)),
        check_vma=False,
    )
```
